32 devices in a mesh: replica: 4 (over x, core), shard: 8 (over z, y).
Axes of the slice: x: 2, y: 2, z: 4, core: 2. Of those that a mesh axis runs over, the one named last changes fastest.
Arguments:
- tokens: bfloat16 [4, 2048, 2048], P('replica', 'shard'), may hold values from -6 to 6
- cotangent: bfloat16 [4, 2048, 2048], P('replica', 'shard'), may hold values from -6 to 6
- lengths: int32 [4], replicated, may hold values from 1024 to 2048, as said below
- attn_gain: bfloat16 [2048], P('shard'), may hold values from 0.5 to 1.5
- query_down: bfloat16 [2048, 1024], P('shard'), may hold values from -0.125 to 0.125
- key_value: bfloat16 [2048, 512], P('shard'), may hold values from -0.125 to 0.125
- query_gain: bfloat16 [1024], P('shard'), may hold values from 0.5 to 1.5
- query_up: bfloat16 [1024, 4096], P('shard'), may hold values from -0.1875 to 0.1875
- out_proj: bfloat16 [4096, 2048], P('shard'), may hold values from -0.75 to 0.75
- mlp_gain: bfloat16 [2048], P('shard'), may hold values from 0.5 to 1.5
- gate_up: bfloat16 [2048, 11264], P('shard'), may hold values from -0.125 to 0.125
- down_proj: bfloat16 [5632, 2048], P('shard'), may hold values from -0.078125 to 0.078125
Outputs:
- layer_out: bfloat16 [4, 2048, 2048], P('replica', 'shard')
- input_grad: bfloat16 [4, 2048, 2048], P('replica', 'shard')
- grad_attn_gain: float32 [2048], P('shard')
- grad_query_down: float32 [2048, 1024], P('shard')
- grad_key_value: float32 [2048, 512], P('shard')
- grad_query_gain: float32 [1024], P('shard')
- grad_query_up: float32 [1024, 4096], P('shard')
- grad_out_proj: float32 [4096, 2048], P('shard')
- grad_mlp_gain: float32 [2048], P('shard')
- grad_gate_up: float32 [2048, 11264], P('shard')
- grad_down_proj: float32 [5632, 2048], P('shard')
The draws below stay inside these ranges and needn't reach their ends.
Inputs may be any that keep to these rules, and one draw needn't show every extreme that they name: `lengths`: real tokens of each sequence, the rest of its slot is padding; some sequence has exactly 2048.
All inputs are finite; a program needn't handle non-finite values.
Results may differ from the reference program's by a relative error of at most 0.022.
Values may be sent and summed in bfloat16 or wider, within the bound.
No kernel may reach another device: no remote copies, remote signals or barrier semaphores. Data moves between devices by JAX's collectives and lax.ppermute only.
A program may use at most 448 MiB of HBM per device.

```python
import math
import jax
import jax.numpy as jnp
from jax import lax

D = 2048
QR = 1024
HEADS = 16
HD = 256
FF = 5632
SLOT = 2048
LEN_MIN = 1024
HQ = 4096
SEQS = 4


def draw_lengths(key, part):
    key_base = jax.random.fold_in(key, 11)
    key_pick = jax.random.fold_in(key, 23)
    drawn = jax.random.randint(key_base, (SEQS,), LEN_MIN, SLOT + 1)
    chosen = jax.random.randint(key_pick, (), 0, SEQS)
    return jnp.where(jnp.arange(SEQS) == chosen, SLOT, drawn).astype(jnp.int32)


def block_scale(rng, shape, cuts, low, top_value):
    level, own = 1.0, jax.random.fold_in(rng, 6)
    for dim, parts in cuts:
        heights = jnp.exp(jax.random.uniform(jax.random.fold_in(own, dim), (parts,), jnp.float32, low / len(cuts), top_value / len(cuts)))
        level = level * jnp.repeat(heights, shape[dim] // parts).reshape([-1 if axis == dim else 1 for axis in range(len(shape))])
    return level


def bell_draw(stream_key, dims, scale, bound, split=(), kind=jnp.bfloat16):
    entries = scale * jax.random.normal(stream_key, dims, jnp.float32)
    if split:
        entries = entries * block_scale(stream_key, dims, split, -0.22, 0.18)
    return jnp.clip(entries, -bound, bound).astype(kind)


def setup_inputs(seed: int = 0) -> dict:
    seeds = jax.random.split(jax.random.key(seed), 13)
    tokens = bell_draw(seeds[0], (SEQS, SLOT, D), 1.0, 6.0, ((0, 4), (1, 8)))
    cotangent = bell_draw(seeds[1], (SEQS, SLOT, D), 1.0, 6.0, ((0, 4), (1, 8)))
    lengths = draw_lengths(jax.random.fold_in(seeds[12], 71), 0)
    attn_gain = jnp.clip(1.0 + 0.1 * jax.random.normal(seeds[3], (D,), jnp.float32), 0.5, 1.5).astype(jnp.bfloat16)
    query_down = bell_draw(seeds[4], (D, QR), D ** -0.5, 0.125, ((0, 8),))
    key_value = bell_draw(seeds[5], (D, 2 * HD), D ** -0.5, 0.125, ((0, 8),))
    query_gain = jnp.clip(1.0 + 0.1 * jax.random.normal(seeds[6], (QR,), jnp.float32), 0.5, 1.5).astype(jnp.bfloat16)
    query_up = bell_draw(seeds[7], (QR, HQ), QR ** -0.5, 0.1875, ((0, 8),))
    out_proj = bell_draw(seeds[8], (HQ, D), (max(HQ // 64, 1)) ** -0.5, 0.75, ((0, 8),))
    mlp_gain = jnp.clip(1.0 + 0.1 * jax.random.normal(seeds[9], (D,), jnp.float32), 0.5, 1.5).astype(jnp.bfloat16)
    gate_up = bell_draw(seeds[10], (D, 2 * FF), D ** -0.5, 0.125, ((0, 8),))
    down_proj = bell_draw(seeds[11], (FF, D), FF ** -0.5, 0.078125, ((0, 8),))
    return dict(tokens=tokens, cotangent=cotangent, lengths=lengths, attn_gain=attn_gain, query_down=query_down, key_value=key_value, query_gain=query_gain, query_up=query_up, out_proj=out_proj, mlp_gain=mlp_gain, gate_up=gate_up, down_proj=down_proj)


EPSILON = 1e-06

@jax.custom_vjp
def low(v):
    return lax.optimization_barrier(v.astype(jnp.bfloat16)).astype(jnp.float32)

@jax.custom_vjp
def low_back(v):
    return v

def low_keep(v):
    return (low(v), None)

def low_pass(kept, grad):
    return (grad,)

def back_keep(v):
    return (v, None)

def back_low(kept, grad):
    return (low(grad),)
low.defvjp(low_keep, low_pass)
low_back.defvjp(back_keep, back_low)

def matmul(left, right):
    return jnp.dot(left, right, precision=lax.Precision.HIGHEST)

def inv_rms(values):
    return lax.rsqrt(lax.optimization_barrier(jnp.mean(values * values, axis=-1, keepdims=True)) + EPSILON)

def rope_tables(positions, head_dim):
    half_dim = head_dim // 2
    frequency = jnp.exp(-math.log(10000.0) * jnp.arange(half_dim).astype(jnp.float32) / half_dim)
    angles = positions.astype(jnp.float32)[:, None] * frequency[None, :]
    return (jnp.cos(angles), jnp.sin(angles))

def rotate(values, cosine, sine):
    half_dim = values.shape[-1] // 2
    first_half = values[..., :half_dim]
    second_half = values[..., half_dim:]
    return jnp.concatenate([first_half * cosine - second_half * sine, second_half * cosine + first_half * sine], axis=-1)

def one_sequence(seq_tokens, seq_length, params):
    first_gain, qdown_mat, kv_mat, query_norm, qup_mat, out_mat, second_gain, gateup_mat, down_mat = params
    scale = 1.0 / math.sqrt(HD)
    positions = jnp.arange(SLOT, dtype=jnp.int32)
    cosine, sine = rope_tables(positions, HD)
    valid = (positions < seq_length).astype(jnp.float32)[:, None]
    normed_first = seq_tokens * inv_rms(seq_tokens)
    attn_input = low(normed_first * first_gain)
    qdown_out = low_back(matmul(attn_input, qdown_mat))
    query_input = low(qdown_out * inv_rms(qdown_out) * query_norm)
    query_raw = low_back(matmul(query_input, qup_mat)).reshape(SLOT, HEADS, HD)
    kv_out = low_back(matmul(attn_input, kv_mat))
    query_rot = low(rotate(query_raw, cosine[:, None, :], sine[:, None, :]))
    key_rot = low(rotate(kv_out[:, :HD], cosine, sine))
    value_part = low(kv_out[:, HD:])
    scores = low_back(jnp.einsum('thd,ud->thu', query_rot, key_rot, precision=lax.Precision.HIGHEST) * scale)
    allowed = (positions[None, :] <= positions[:, None]) & (positions[None, :] < seq_length)
    scores = jnp.where(allowed[:, None, :], scores, -1e+30)
    probs = low(jax.nn.softmax(scores, axis=-1))
    attn_val = jnp.einsum('thu,ud->thd', probs, value_part, precision=lax.Precision.HIGHEST).reshape(SLOT, HEADS * HD)
    attn_low = low(low_back(attn_val))
    middle = seq_tokens + low_back(matmul(attn_low, out_mat))
    normed_second = middle * inv_rms(middle)
    mlp_input = low(normed_second * second_gain)
    gateup_out = low_back(matmul(mlp_input, gateup_mat))
    hidden_low = low(jax.nn.silu(gateup_out[:, :FF]) * gateup_out[:, FF:])
    return (middle + matmul(hidden_low, down_mat)) * valid

def reference(tokens, cotangent, lengths, attn_gain, query_down, key_value, query_gain, query_up, out_proj, mlp_gain, gate_up, down_proj):
    inputs = tokens.astype(jnp.float32)
    params = tuple((weight.astype(jnp.float32) for weight in (attn_gain, query_down, key_value, query_gain, query_up, out_proj, mlp_gain, gate_up, down_proj)))

    def forward(seq_inputs, param_tuple):

        def seq_step(seq_pair):
            return one_sequence(seq_pair[0], seq_pair[1], param_tuple)
        return lax.map(jax.checkpoint(seq_step), (seq_inputs, lengths))
    layer, pullback = jax.vjp(forward, inputs, params)
    input_grad, param_grads = pullback(cotangent.astype(jnp.float32))
    return (layer.astype(jnp.bfloat16), input_grad.astype(jnp.bfloat16), param_grads[0], param_grads[1], param_grads[2], param_grads[3], param_grads[4], param_grads[5], param_grads[6], param_grads[7], param_grads[8])
```

```python
import math

import jax
import jax.numpy as jnp
from jax import lax
from jax.experimental import pallas as pl
from jax.experimental.pallas import tpu as pltpu
from jax.sharding import Mesh
from jax.sharding import PartitionSpec as P

HEADS = 16
HD = 256
FF = 5632
Z = 4
CORES = 2


EPSILON = 1e-06
BF = jnp.bfloat16
F32 = jnp.float32


def inv_rms(values):
    return lax.rsqrt(jnp.mean(values * values, axis=-1, keepdims=True) + EPSILON)


def rope_tables(positions, head_dim):
    half_dim = head_dim // 2
    frequency = jnp.exp(-math.log(10000.0) * jnp.arange(half_dim).astype(F32) / half_dim)
    angles = positions.astype(F32)[:, None] * frequency[None, :]
    return (jnp.cos(angles), jnp.sin(angles))


def rotate(values, cosine, sine):
    half_dim = values.shape[-1] // 2
    first_half = values[..., :half_dim]
    second_half = values[..., half_dim:]
    return jnp.concatenate(
        [first_half * cosine - second_half * sine, second_half * cosine + first_half * sine],
        axis=-1,
    )


def rotate_back(grads, cosine, sine):
    half_dim = grads.shape[-1] // 2
    first_half = grads[..., :half_dim]
    second_half = grads[..., half_dim:]
    return jnp.concatenate(
        [first_half * cosine + second_half * sine, second_half * cosine - first_half * sine],
        axis=-1,
    )


def matmul(left, right):
    return jnp.dot(left, right, preferred_element_type=F32)


def contract_rows(left, right):
    return lax.dot_general(left, right, (((0,), (0,)), ((), ())), preferred_element_type=F32)


def contract_cols(left, right):
    return lax.dot_general(left, right, (((1,), (1,)), ((), ())), preferred_element_type=F32)


STEP_HEADS = 2
NEG = -1e30


def dot_last(left, right):
    return lax.dot_general(left, right, (((1,), (1,)), ((), ())), preferred_element_type=F32)


def seen(shape, rows, y_index):
    n_y = shape[0] // rows
    key = lax.broadcasted_iota(jnp.int32, shape, 0)
    row = lax.broadcasted_iota(jnp.int32, shape, 1)
    ahead = key // rows
    block = lax.rem(y_index + ahead, n_y)
    return (block - y_index) * rows + key - ahead * rows <= row


def attend_kernel(
    place_ref, input_ref, up_ref, cos_ref, sin_ref, kv_ref, q_ref, o_ref, lse_ref,
    vt_ref, m_ref, l_ref, acc_ref,
):
    rows = input_ref.shape[0]
    chunk_rows = kv_ref.shape[0] // Z
    half = HD // 2

    @pl.when(pl.program_id(0) == 0)
    def _():
        for c in range(Z):
            at = slice(c * chunk_rows, (c + 1) * chunk_rows)
            vt_ref[:, at] = kv_ref[at, HD:].T

    cosine, sine = cos_ref[...], sin_ref[...]
    scale = 1.0 / math.sqrt(HD)
    raw = matmul(input_ref[...], up_ref[...])
    for j in range(STEP_HEADS):
        first, second = raw[:, j * HD : j * HD + half], raw[:, j * HD + half : (j + 1) * HD]
        turned = jnp.concatenate(
            [first * cosine - second * sine, second * cosine + first * sine], axis=1
        )
        q_ref[:, j * HD : (j + 1) * HD] = (turned.astype(BF).astype(F32) * scale).astype(BF)
    m_ref[...] = jnp.full_like(m_ref, NEG)
    l_ref[...] = jnp.zeros_like(l_ref)
    acc_ref[...] = jnp.zeros_like(acc_ref)

    def chunk(c, masked):
        at = pl.multiple_of(c * chunk_rows, chunk_rows)
        keys = kv_ref[pl.ds(at, chunk_rows), :HD]
        values = vt_ref[:, pl.ds(at, chunk_rows)]
        for j in range(STEP_HEADS):
            scores = dot_last(keys, q_ref[:, j * HD : (j + 1) * HD])
            if masked:
                scores = jnp.where(seen(scores.shape, rows, place_ref[1]), scores, NEG)
            peak = jnp.maximum(m_ref[j], jnp.max(scores, axis=0, keepdims=True))
            alpha = jnp.exp(m_ref[j] - peak)
            expo = jnp.exp(scores - peak)
            m_ref[j] = peak
            l_ref[j] = l_ref[j] * alpha + jnp.sum(expo, axis=0, keepdims=True)
            acc_ref[j] = acc_ref[j] * alpha + matmul(values, expo.astype(BF))

    @pl.loop(Z - place_ref[0], Z)
    def _(c):
        chunk(c, False)

    chunk(0, True)
    for j in range(STEP_HEADS):
        o_ref[:, j * HD : (j + 1) * HD] = (acc_ref[j] / l_ref[j]).T.astype(BF)
        lse_ref[j] = m_ref[j] + jnp.log(l_ref[j])


def attend(place, query_input, up_mat, cosine, sine, kv_whole):
    rows, rank = query_input.shape
    slot_len = kv_whole.shape[0]
    wide = STEP_HEADS * HD
    whole = lambda h, *_: (0, 0)
    by_head = lambda h, *_: (0, h)
    flops = 2 * rows * HEADS * HD * (rank + 2 * slot_len)
    return pl.pallas_call(
        attend_kernel,
        out_shape=(
            jax.ShapeDtypeStruct((rows, HEADS * HD), BF),
            jax.ShapeDtypeStruct((rows, HEADS * HD), BF),
            jax.ShapeDtypeStruct((HEADS, 1, rows), F32),
        ),
        grid_spec=pltpu.PrefetchScalarGridSpec(
            num_scalar_prefetch=1,
            grid=(HEADS // STEP_HEADS,),
            in_specs=[
                pl.BlockSpec((rows, rank), whole),
                pl.BlockSpec((rank, wide), by_head),
                pl.BlockSpec((rows, HD // 2), whole),
                pl.BlockSpec((rows, HD // 2), whole),
                pl.BlockSpec((slot_len, 2 * HD), whole),
            ],
            out_specs=[
                pl.BlockSpec((rows, wide), by_head),
                pl.BlockSpec((rows, wide), by_head),
                pl.BlockSpec((STEP_HEADS, 1, rows), lambda h, *_: (h, 0, 0)),
            ],
            scratch_shapes=[
                pltpu.VMEM((HD, slot_len), BF),
                pltpu.VMEM((STEP_HEADS, 1, rows), F32),
                pltpu.VMEM((STEP_HEADS, 1, rows), F32),
                pltpu.VMEM((STEP_HEADS, HD, rows), F32),
            ],
        ),
        compiler_params=pltpu.CompilerParams(
            dimension_semantics=("arbitrary",), vmem_limit_bytes=40 * 1024 * 1024
        ),
        cost_estimate=pl.CostEstimate(
            flops=flops,
            bytes_accessed=2 * (rank + 3 * rows) * HEADS * HD,
            transcendentals=rows * HEADS * slot_len,
        ),
    )(place, query_input, up_mat, cosine, sine, kv_whole)


def attend_back_kernel(
    place_ref, q_ref, do_ref, o_ref, lse_ref, cos_ref, sin_ref, kv_ref, dq_ref, dkv_ref,
    acc_ref, dqs_ref,
):
    rows = q_ref.shape[0]
    chunk_rows = kv_ref.shape[0] // Z
    half = HD // 2
    step = pl.program_id(0)

    @pl.when(step == 0)
    def _():
        acc_ref[...] = jnp.zeros_like(acc_ref)

    dqs_ref[...] = jnp.zeros_like(dqs_ref)
    deltas = []
    for j in range(STEP_HEADS):
        at = slice(j * HD, (j + 1) * HD)
        prod = do_ref[:, at].astype(F32) * o_ref[:, at].astype(F32)
        deltas.append(jnp.sum(prod.T, axis=0, keepdims=True))

    def chunk(c, masked):
        at = pl.ds(pl.multiple_of(c * chunk_rows, chunk_rows), chunk_rows)
        keys = kv_ref[at, :HD]
        values = kv_ref[at, HD:]
        for j in range(STEP_HEADS):
            query = q_ref[:, j * HD : (j + 1) * HD]
            out_grad = do_ref[:, j * HD : (j + 1) * HD]
            probs = jnp.exp(dot_last(keys, query) - lse_ref[j])
            if masked:
                probs = jnp.where(seen(probs.shape, rows, place_ref[1]), probs, 0.0)
            score_grad = (probs * (dot_last(values, out_grad) - deltas[j])).astype(BF)
            acc_ref[at, HD:] += matmul(probs.astype(BF), out_grad)
            acc_ref[at, :HD] += matmul(score_grad, query)
            dqs_ref[j] += contract_rows(score_grad, keys)

    @pl.loop(Z - place_ref[0], Z)
    def _(c):
        chunk(c, False)

    chunk(0, True)
    cosine, sine = cos_ref[...], sin_ref[...]
    scale = 1.0 / math.sqrt(HD)
    for j in range(STEP_HEADS):
        first, second = dqs_ref[j, :, :half] * scale, dqs_ref[j, :, half:] * scale
        dq_ref[:, j * HD : (j + 1) * HD] = jnp.concatenate(
            [first * cosine + second * sine, second * cosine - first * sine], axis=1
        ).astype(BF)

    @pl.when(step == pl.num_programs(0) - 1)
    def _():
        dkv_ref[...] = acc_ref[...].astype(BF)


def attend_back(place, query, out_grad, attn_low, logsum, cosine, sine, kv_whole):
    rows = query.shape[0]
    slot_len = kv_whole.shape[0]
    wide = STEP_HEADS * HD
    whole = lambda h, *_: (0, 0)
    by_head = lambda h, *_: (0, h)
    return pl.pallas_call(
        attend_back_kernel,
        out_shape=(
            jax.ShapeDtypeStruct((rows, HEADS * HD), BF),
            jax.ShapeDtypeStruct((slot_len, 2 * HD), BF),
        ),
        grid_spec=pltpu.PrefetchScalarGridSpec(
            num_scalar_prefetch=1,
            grid=(HEADS // STEP_HEADS,),
            in_specs=[
                pl.BlockSpec((rows, wide), by_head),
                pl.BlockSpec((rows, wide), by_head),
                pl.BlockSpec((rows, wide), by_head),
                pl.BlockSpec((STEP_HEADS, 1, rows), lambda h, *_: (h, 0, 0)),
                pl.BlockSpec((rows, HD // 2), whole),
                pl.BlockSpec((rows, HD // 2), whole),
                pl.BlockSpec((slot_len, 2 * HD), whole),
            ],
            out_specs=[
                pl.BlockSpec((rows, wide), by_head),
                pl.BlockSpec((slot_len, 2 * HD), whole),
            ],
            scratch_shapes=[
                pltpu.VMEM((slot_len, 2 * HD), F32),
                pltpu.VMEM((STEP_HEADS, rows, HD), F32),
            ],
        ),
        compiler_params=pltpu.CompilerParams(
            dimension_semantics=("arbitrary",), vmem_limit_bytes=40 * 1024 * 1024
        ),
        cost_estimate=pl.CostEstimate(
            flops=10 * rows * HEADS * HD * slot_len,
            bytes_accessed=2 * 4 * rows * HEADS * HD,
            transcendentals=rows * HEADS * slot_len,
        ),
    )(place, query, out_grad, attn_low, logsum, cosine, sine, kv_whole)


def interleave_kernel(n_shard, order_ref, gain_ref, weight_ref, *refs):
    *slot_refs, out_ref, sum_ref = refs
    n_group = len(slot_refs)
    slots = [ref[...].astype(F32) for ref in slot_refs]
    part = slots[0].shape[1] // 2
    unit = part // n_shard
    width = part * n_group
    blocks = []
    for member in range(n_group):
        block = slots[0]
        for k in range(1, n_group):
            block = jnp.where(order_ref[member] == k, slots[k], block)
        blocks.append(block)
    total = 0.0
    gain = gain_ref[...]
    for half in range(2):
        row = jnp.concatenate(
            [
                blocks[member][:, half * part + s * unit : half * part + (s + 1) * unit]
                for s in range(n_shard)
                for member in range(n_group)
            ],
            axis=1,
        )
        at = slice(half * width, (half + 1) * width)
        total = total + jnp.sum(row * weight_ref[:, at].astype(F32), axis=1, keepdims=True)
        out_ref[:, at] = row * gain
    sum_ref[...] = total


def interleave(order, gain, weight, slots, n_shard):
    rows, width = weight.shape
    block = 32
    by_row = lambda i, *_: (i, 0)
    return pl.pallas_call(
        lambda *refs: interleave_kernel(n_shard, *refs),
        out_shape=(
            jax.ShapeDtypeStruct((rows, width), F32),
            jax.ShapeDtypeStruct((rows, 1), F32),
        ),
        grid_spec=pltpu.PrefetchScalarGridSpec(
            num_scalar_prefetch=1,
            grid=(rows // block,),
            in_specs=[
                pl.BlockSpec((block, 1), by_row),
                pl.BlockSpec((block, width), by_row),
                *[pl.BlockSpec((block, slots[0].shape[1]), by_row) for _ in slots],
            ],
            out_specs=[
                pl.BlockSpec((block, width), by_row),
                pl.BlockSpec((block, 1), by_row),
            ],
        ),
        compiler_params=pltpu.CompilerParams(dimension_semantics=("arbitrary",)),
        cost_estimate=pl.CostEstimate(
            flops=4 * rows * width, bytes_accessed=8 * rows * width, transcendentals=0
        ),
    )(order, gain, weight, *slots)


def from_ahead(value, axis, step):
    n = lax.axis_size(axis)
    return lax.ppermute(value, axis, [((j + step) % n, j) for j in range(n)])


def to_ahead(value, axis, step):
    n = lax.axis_size(axis)
    return lax.ppermute(value, axis, [(j, (j + step) % n) for j in range(n)])


def gather_group(value):
    n_x = lax.axis_size("x")
    mine = [value] + [from_ahead(value, "x", k) for k in range(1, n_x)]
    return mine + [from_ahead(v, "c", 1) for v in mine]


def reduce_group(parts):
    n_x = lax.axis_size("x")
    near, far = parts[:n_x], parts[n_x:]
    sums = [a + to_ahead(b.astype(BF), "c", 1).astype(F32) for a, b in zip(near, far)]
    total = sums[0]
    for k in range(1, n_x):
        total = total + to_ahead(sums[k].astype(BF), "x", k).astype(F32)
    return total


def exchange_group(value, pick):
    n_x = lax.axis_size("x")
    x_id, c_id = lax.axis_index("x"), lax.axis_index("c")
    out = []
    for dc in range(CORES):
        for dx in range(n_x):
            member = lax.rem(x_id + n_x - dx, n_x) * CORES + lax.rem(c_id + dc, CORES)
            block = pick(value, member)
            if dx or dc:
                perm = []
                for j in range(n_x):
                    for c in range(CORES):
                        source = ((j + dx) % n_x) * CORES + (c + dc) % CORES
                        perm.append((source, j * CORES + c))
                block = lax.ppermute(block, ("x", "c"), perm)
            out.append(block)
    return out


def shard_offsets():
    return [(dz, dy) for dz in range(Z) for dy in range(lax.axis_size("y"))]


def shard_permute(value, dz, dy, ahead):
    n_y = lax.axis_size("y")
    perm = []
    for z in range(Z):
        for y in range(n_y):
            far, near = ((z + dz) % Z) * n_y + (y + dy) % n_y, z * n_y + y
            perm.append((near, far) if ahead else (far, near))
    return lax.ppermute(value, ("z", "y"), perm)


def position_of(dz, dy):
    n_y = lax.axis_size("y")
    return lax.rem(lax.axis_index("z") + dz, Z) * n_y + lax.rem(lax.axis_index("y") + dy, n_y)


def ring_z(value):
    return [from_ahead(value, "z", k) if k else value for k in range(Z)]


def scatter_small(blocks):
    near = blocks[0]
    total = jnp.stack(near).astype(F32)
    for k, group in enumerate(blocks[1:]):
        total = total + to_ahead(jnp.stack(group).astype(BF), "y", k + 1).astype(F32)
    out = total[0]
    low = total.astype(BF)
    for k in range(1, Z):
        out = out + to_ahead(low[k], "z", k).astype(F32)
    return out


def after(values, done):
    return lax.optimization_barrier((values, done))[0]


def gather_z(value):
    return lax.all_gather(value, "z", axis=0, tiled=True)


def gather_shard(value):
    return lax.all_gather(value, ("z", "y"), axis=0, tiled=True)


def scatter_z(value):
    return lax.psum_scatter(value, "z", scatter_dimension=0, tiled=True)


def begin_reduce_y(value):
    n_y = lax.axis_size("y")
    index = lax.axis_index("y")
    blocks = value.astype(BF).reshape(Z, n_y, -1, value.shape[1])
    own = lax.dynamic_index_in_dim(blocks, index, axis=1, keepdims=False)
    others = []
    for k in range(1, n_y):
        block = lax.dynamic_index_in_dim(blocks, lax.rem(index + k, n_y), axis=1, keepdims=False)
        others.append(to_ahead(block, "y", k))
    return own, others


def end_reduce_y(own, others):
    total = own.astype(F32)
    for block in others:
        total = total + block.astype(F32)
    return total.astype(BF).reshape(-1, own.shape[-1])


def swap_y(wide):
    n_y = lax.axis_size("y")
    return [wide] + [from_ahead(wide, "y", k) for k in range(1, n_y)]


def merge_y(blocks, n):
    n_y = lax.axis_size("y")
    m = blocks[0].shape[1]
    blocks = [block.reshape(Z, 1, n, m) for block in blocks]
    if n_y == 2:
        first, second = blocks
        return jnp.where(
            lax.axis_index("y") == 0,
            jnp.concatenate([first, second], axis=1),
            jnp.concatenate([second, first], axis=1),
        ).reshape(-1, m)
    at = lax.rem(n_y - lax.axis_index("y"), n_y)
    stacked = jnp.concatenate(blocks + blocks[:-1], axis=1)
    return lax.dynamic_slice_in_dim(stacked, at, n_y, axis=1).reshape(-1, m)


def merge_own_y(blocks):
    n_y = lax.axis_size("y")
    if n_y == 2:
        first, second = blocks
        return jnp.where(
            lax.axis_index("y") == 0,
            jnp.concatenate([first, second]),
            jnp.concatenate([second, first]),
        )
    n = blocks[0].shape[0]
    at = lax.rem(n_y - lax.axis_index("y"), n_y) * n
    return lax.dynamic_slice_in_dim(jnp.concatenate(blocks + blocks[:-1]), at, n_y * n)


def reduce_own_y(value):
    n_y = lax.axis_size("y")
    index = lax.axis_index("y")
    blocks = value.reshape(n_y, -1, value.shape[1])
    total = lax.dynamic_index_in_dim(blocks, index, keepdims=False).astype(F32)
    for k in range(1, n_y):
        other = lax.dynamic_index_in_dim(blocks, lax.rem(index + k, n_y), keepdims=False)
        total = total + to_ahead(other, "y", k).astype(F32)
    return total.astype(BF)


def member_of(dc, dx):
    n_x = lax.axis_size("x")
    x_id = lax.rem(lax.axis_index("x") + dx, n_x)
    return x_id * CORES + lax.rem(lax.axis_index("c") + dc, CORES)


def offsets():
    return [(dc, dx) for dc in range(CORES) for dx in range(lax.axis_size("x"))]


def place_group(slots, axis, dtype):
    n = slots[0].shape[axis]
    shape = list(slots[0].shape)
    shape[axis] = n * len(slots)
    out = jnp.zeros(shape, dtype)
    for (dc, dx), slot in zip(offsets(), slots):
        start = [0] * len(shape)
        start[axis] = member_of(dc, dx) * n
        out = lax.dynamic_update_slice(out, slot.astype(dtype), start)
    return out


def spread_begin(wide):
    n_y, n_x = lax.axis_size("y"), lax.axis_size("x")
    over_y = [wide] + [from_ahead(wide, "y", k) for k in range(1, n_y)]
    over_x = [from_ahead(wide, "x", k) for k in range(1, n_x)]
    return over_y, over_x


def spread_next(over_y, over_x):
    n_x = lax.axis_size("x")
    return [[over_y[0]] + over_x] + [
        [block] + [from_ahead(block, "x", k) for k in range(1, n_x)] for block in over_y[1:]
    ]


def spread_end(grid):
    return [group + [from_ahead(block, "c", 1) for block in group] for group in grid]


def place_every(slots, n):
    n_y, n_x = lax.axis_size("y"), lax.axis_size("x")
    m = slots[0][0].shape[1]
    out = jnp.zeros((Z, n_y, n_x * CORES, n, m), BF)
    for ky, group in enumerate(slots):
        at_y = lax.rem(lax.axis_index("y") + ky, n_y)
        for (dc, dx), slot in zip(offsets(), group):
            out = lax.dynamic_update_slice(
                out, slot.reshape(Z, 1, 1, n, m), (0, at_y, member_of(dc, dx), 0, 0)
            )
    return out.reshape(-1, m)


def on_device(
    tokens,
    cotangent,
    lengths,
    attn_gain,
    query_down,
    key_value,
    query_gain,
    query_up,
    out_proj,
    mlp_gain,
    gate_up,
    down_proj,
):
    n_x = lax.axis_size("x")
    n_group = n_x * CORES
    n_y = lax.axis_size("y")
    n_shard = Z * n_y
    _, rows, width = tokens.shape
    rank = query_down.shape[1]
    group_id = lax.axis_index("x") * CORES + lax.axis_index("c")
    shard_id = lax.axis_index("z") * n_y + lax.axis_index("y")

    def quarter_rows(value):
        n = value.shape[0] // n_group
        return lax.dynamic_slice_in_dim(value, group_id * n, n, axis=0)

    def pick_cols(value, member):
        n = value.shape[1] // n_group
        return lax.dynamic_slice_in_dim(value, member * n, n, axis=1)

    def scaled(weight, gain):
        return (weight.astype(F32) * gain.astype(F32)[:, None]).astype(BF)

    def split(value):
        return [value[k * rows : (k + 1) * rows] for k in range(n_group)]

    qkv_own = jnp.concatenate([query_down, key_value], axis=1)
    qkv_ring = ring_z(scaled(pick_cols(qkv_own, group_id), attn_gain))
    qup_wide = gather_z(quarter_rows(scaled(query_up, query_gain)))
    out_wide = gather_z(quarter_rows(out_proj))
    unit = FF // n_shard // n_group
    part = FF // n_group

    my_length = lax.dynamic_index_in_dim(lengths, group_id, keepdims=False)
    positions = shard_id * rows + jnp.arange(rows, dtype=jnp.int32)
    place = jnp.stack([lax.axis_index("z"), lax.axis_index("y")]).astype(jnp.int32)
    valid = (positions < my_length).astype(F32)[:, None]
    cosine, sine = rope_tables(positions, HD)

    x_rows = tokens[0].astype(F32)
    rms_first = inv_rms(x_rows)
    normed_first = x_rows * rms_first
    attn_input = normed_first.astype(BF)
    input_all = jnp.concatenate(gather_group(attn_input), axis=0)

    qkv_stack = jnp.stack(qkv_ring)
    qkv_grid = [qkv_stack] + [from_ahead(qkv_stack, "y", k) for k in range(1, n_y)]

    gate_up_late = after(gate_up, qkv_stack)
    gu_parts = gate_up_late.reshape(gate_up.shape[0], 2, n_shard, n_group, unit)
    gu_own = lax.dynamic_index_in_dim(gu_parts, group_id, axis=3, keepdims=False)
    gu_own = scaled(gu_own.reshape(-1, 2 * part), mlp_gain)
    gate_own, up_own = gu_own[:, :part], gu_own[:, part:]
    gate_wide = gather_z(gate_own)

    qup_first = spread_begin(qup_wide)
    qkv_mat = jnp.zeros((width, qkv_stack.shape[2]), BF)
    for dy, stack in enumerate(after(qkv_grid, qup_wide)):
        for dz in range(Z):
            at = position_of(dz, dy) * stack.shape[1]
            qkv_mat = lax.dynamic_update_slice(qkv_mat, stack[dz], (at, 0))
    qkv_flat = matmul(input_all, qkv_mat)
    up_wide = gather_z(up_own)
    blocks = []
    for (dc, dx), block in zip(offsets(), split(qkv_flat)):
        if dc or dx:
            perm = []
            for j in range(n_x):
                for c in range(CORES):
                    target = ((j + dx) % n_x) * CORES + (c + dc) % CORES
                    perm.append((j * CORES + c, target))
            block = lax.ppermute(block, ("x", "c"), perm)
        blocks.append(block)
    qup_grid = spread_next(*qup_first)
    blocks = after(blocks, qup_first)
    qkv_out = jnp.zeros((rows, qkv_own.shape[1]), F32)
    n_cols = qkv_own.shape[1] // n_group
    for (dc, dx), block in zip(offsets(), blocks):
        member = lax.rem(lax.axis_index("x") + n_x - dx, n_x) * CORES
        member = member + lax.rem(lax.axis_index("c") + dc, CORES)
        qkv_out = lax.dynamic_update_slice(qkv_out, block, (0, member * n_cols))
    qdown_out, kv_out = qkv_out[:, :rank], qkv_out[:, rank:]

    key_rot = rotate(kv_out[:, :HD], cosine, sine).astype(BF)
    kv_local = jnp.concatenate([key_rot, kv_out[:, HD:].astype(BF)], axis=1)
    out_first = spread_begin(out_wide)
    kv_local = after(kv_local, out_wide)
    kv_ring = ring_z(kv_local)
    down_both = [quarter_rows(down_proj)]
    down_both += [from_ahead(after(down_both[0], qkv_flat), "y", k) for k in range(1, n_y)]
    down_mat = gather_z(merge_own_y(down_both))
    rms_query = inv_rms(qdown_out)
    normed_query = qdown_out * rms_query
    query_input = normed_query.astype(BF)
    qup_slots = spread_end(qup_grid)
    kv_stack = jnp.stack(after(kv_ring, qup_grid))
    kv_grid = [kv_stack] + [from_ahead(kv_stack, "y", k) for k in range(1, n_y)]
    qup_mat = place_every(after(qup_slots, kv_stack), query_up.shape[0] // n_group)
    kv_grid = after(kv_grid, qup_mat)
    kv_whole = jnp.concatenate([stack[dz] for dz in range(Z) for stack in kv_grid])
    query_late = after(query_input, out_first)
    out_grid = spread_next(*out_first)
    query_rot, attn_low, logsum = attend(place, query_late, qup_mat, cosine, sine, kv_whole)
    gate_blocks = swap_y(after(gate_wide, attn_low))
    out_mat = place_every(after(spread_end(out_grid), attn_low), out_proj.shape[0] // n_group)
    middle = x_rows + matmul(attn_low, out_mat)
    rms_second = inv_rms(middle)
    normed_second = middle * rms_second
    mlp_input = normed_second.astype(BF)

    mlp_all = jnp.concatenate(gather_group(mlp_input), axis=0)
    up_blocks = swap_y(after(up_wide, mlp_input))
    cot_rows = cotangent[0].astype(F32) * valid
    cot_late = after(cot_rows.astype(BF), mlp_input)
    cot_all = jnp.concatenate(gather_group(cot_late), axis=0)
    gate_mat = merge_y(after(gate_blocks, mlp_all), mlp_gain.shape[0])
    gate_part = matmul(mlp_all, gate_mat)
    up_mat = merge_y(after(up_blocks, (gate_part, down_mat)), mlp_gain.shape[0])
    up_part = matmul(mlp_all, up_mat)
    sigmoid_gate = jax.nn.sigmoid(gate_part)
    activated = gate_part * sigmoid_gate
    hidden_low = (activated * up_part).astype(BF)

    def pick_out(value, member):
        parts = value.reshape(rows, n_shard, n_group, -1)
        return lax.dynamic_index_in_dim(parts, member, axis=2, keepdims=False).reshape(rows, -1)

    attn_late, query_late = after((attn_low, query_input), cot_all)
    attn_all = jnp.concatenate(exchange_group(attn_late, pick_out), axis=0)
    query_all = jnp.concatenate(gather_group(query_late), axis=0)

    down_term = contract_rows(hidden_low, cot_all).astype(BF)
    down_half = scatter_z(down_term)
    down_mat = after(down_mat, (down_term, attn_all, query_all))
    hidden_grad = contract_cols(cot_all, down_mat)
    gate_grad = hidden_grad * up_part * (sigmoid_gate * (1.0 + gate_part * (1.0 - sigmoid_gate)))
    gate_low = gate_grad.astype(BF)
    up_low = (hidden_grad * activated).astype(BF)
    partial_in = contract_cols(gate_low, gate_mat) + contract_cols(up_low, up_mat)
    gate_low, up_low = after((gate_low, up_low), partial_in)
    gate_term = contract_rows(mlp_all, gate_low).astype(BF)
    gate_ends = begin_reduce_y(gate_term)
    up_term = contract_rows(mlp_all, after(up_low, gate_term)).astype(BF)
    up_ends = begin_reduce_y(up_term)
    mlp_in_grad = after(reduce_group(split(partial_in)), up_term)

    middle_grad = cot_rows + rms_second * (
        mlp_in_grad
        - normed_second * jnp.mean(mlp_in_grad * normed_second, axis=-1, keepdims=True)
    )
    middle_low = middle_grad.astype(BF)
    middle_all = jnp.concatenate(gather_group(middle_low), axis=0)
    attn_val_grad = contract_cols(middle_low, out_mat).astype(BF)
    query_raw_grad, kv_term = attend_back(
        place, query_rot, attn_val_grad, attn_low, logsum, cosine, sine, kv_whole
    )
    kv_slots = [kv_term[k * rows : (k + 1) * rows] for k in range(Z * n_y)]
    kv_grad = scatter_small([kv_slots[k::n_y] for k in range(n_y)])
    gate_pre = end_reduce_y(gate_ends[0], after(gate_ends[1], kv_term))
    gate_sum = scatter_z(gate_pre)
    out_term = contract_rows(attn_all, after(middle_all, gate_pre)).astype(BF)
    out_ends = begin_reduce_y(out_term)
    raw_all = jnp.concatenate(exchange_group(query_raw_grad, pick_cols), axis=0)
    query_in_grad = contract_cols(query_raw_grad, qup_mat)
    qup_term = contract_rows(query_all, raw_all).astype(BF)
    qup_ends = begin_reduce_y(qup_term)
    hidden_late = after(hidden_low, (qup_term, out_term))
    layer_part = matmul(hidden_late, down_mat)
    layer = (middle + reduce_group(split(layer_part))) * valid
    qdown_grad = rms_query * (
        query_in_grad
        - normed_query * jnp.mean(query_in_grad * normed_query, axis=-1, keepdims=True)
    )
    kv_grad = after(kv_grad, down_half)
    key_raw_grad = rotate_back(kv_grad[:, :HD], cosine, sine)
    qkv_low = jnp.concatenate([qdown_grad, key_raw_grad, kv_grad[:, HD:]], axis=1).astype(BF)
    qkv_all = jnp.concatenate(exchange_group(qkv_low, pick_cols), axis=0)
    qkv_term = contract_rows(input_all, qkv_all).astype(BF)
    n_own = query_down.shape[0]
    qkv_sum = scatter_small(
        [
            [
                lax.dynamic_slice_in_dim(qkv_term, position_of(dz, dy) * n_own, n_own)
                for dz in range(Z)
            ]
            for dy in range(n_y)
        ]
    ).astype(BF)
    down_sum = reduce_own_y(down_half)
    first_part = contract_cols(after(qkv_all, qkv_term), qkv_mat)
    up_pre = end_reduce_y(up_ends[0], after(up_ends[1], (qkv_low, layer_part)))
    up_sum = scatter_z(up_pre)
    out_pre = end_reduce_y(out_ends[0], after(out_ends[1], (up_pre, first_part)))
    out_sum = scatter_z(out_pre)
    qup_pre = end_reduce_y(qup_ends[0], after(qup_ends[1], out_pre))
    qup_sum = scatter_z(qup_pre)
    first_in_grad = reduce_group(split(first_part))
    input_rows_grad = middle_grad + rms_first * (
        first_in_grad
        - normed_first * jnp.mean(first_in_grad * normed_first, axis=-1, keepdims=True)
    )

    down_grad = place_group(gather_group(down_sum), 0, F32)
    gate_sum = after(gate_sum, down_grad)
    up_sum = after(up_sum, gate_sum)
    gateup_slots = gather_group(jnp.concatenate([gate_sum, up_sum], axis=1))
    out_sum = after(out_sum, up_sum)
    out_grad = place_group(gather_group(out_sum), 0, F32)
    qup_sum = after(qup_sum, out_sum)
    order = jnp.zeros((n_group,), jnp.int32)
    for k, (dc, dx) in enumerate(offsets()):
        order = order.at[member_of(dc, dx)].set(k)
    gateup_grad, second_gain_grad = interleave(
        order, mlp_gain.astype(F32)[:, None], gate_up, gateup_slots, n_shard
    )
    qup_raw = place_group(gather_group(qup_sum), 1, F32)
    qkv_raw = place_group(gather_group(qkv_sum), 1, F32)

    def gain_grad(weight, grad):
        return jnp.sum(weight.astype(F32) * grad, axis=1)

    qkv_weight_grad = qkv_raw * attn_gain.astype(F32)[:, None]
    return (
        layer.astype(BF)[None],
        input_rows_grad.astype(BF)[None],
        gain_grad(qkv_own, qkv_raw),
        qkv_weight_grad[:, :rank],
        qkv_weight_grad[:, rank:],
        gain_grad(query_up, qup_raw),
        qup_raw * query_gain.astype(F32)[:, None],
        out_grad,
        second_gain_grad[:, 0],
        gateup_grad,
        down_grad,
    )


def solution(mesh):
    n_replica, n_shard = mesh.devices.shape
    devices = mesh.devices.reshape(n_replica // CORES, CORES, Z, n_shard // Z)
    inner = Mesh(devices, ("x", "c", "z", "y"))
    group, shard = ("x", "c"), ("z", "y")
    acts = P(group, shard, None)
    vec = P(shard)
    mat = P(shard, None)
    in_specs = (acts, acts, P(), vec, mat, mat, vec, mat, mat, vec, mat, mat)
    out_specs = (acts, acts, vec, mat, mat, vec, mat, mat, vec, mat, mat)
    return jax.shard_map(
        on_device, mesh=inner, in_specs=in_specs, out_specs=out_specs, check_vma=False
    )
```

```python
import math

import jax
import jax.numpy as jnp
from jax import lax
from jax.experimental import pallas as pl
from jax.experimental.pallas import tpu as pltpu
from jax.sharding import Mesh
from jax.sharding import PartitionSpec as P

HEADS = 16
HD = 256
FF = 5632
Z = 4
CORES = 2


EPSILON = 1e-06
BF = jnp.bfloat16
F32 = jnp.float32


def inv_rms(values):
    return lax.rsqrt(jnp.mean(values * values, axis=-1, keepdims=True) + EPSILON)


def rope_tables(positions, head_dim):
    half_dim = head_dim // 2
    frequency = jnp.exp(-math.log(10000.0) * jnp.arange(half_dim).astype(F32) / half_dim)
    angles = positions.astype(F32)[:, None] * frequency[None, :]
    return (jnp.cos(angles), jnp.sin(angles))


def rotate(values, cosine, sine):
    half_dim = values.shape[-1] // 2
    first_half = values[..., :half_dim]
    second_half = values[..., half_dim:]
    return jnp.concatenate(
        [first_half * cosine - second_half * sine, second_half * cosine + first_half * sine],
        axis=-1,
    )


def rotate_back(grads, cosine, sine):
    half_dim = grads.shape[-1] // 2
    first_half = grads[..., :half_dim]
    second_half = grads[..., half_dim:]
    return jnp.concatenate(
        [first_half * cosine + second_half * sine, second_half * cosine - first_half * sine],
        axis=-1,
    )


def matmul(left, right):
    return jnp.dot(left, right, preferred_element_type=F32)


def contract_rows(left, right):
    return lax.dot_general(left, right, (((0,), (0,)), ((), ())), preferred_element_type=F32)


def contract_cols(left, right):
    return lax.dot_general(left, right, (((1,), (1,)), ((), ())), preferred_element_type=F32)


STEP_HEADS = 2
LIGHT = 1000
NEG = -1e30


def dot_last(left, right):
    return lax.dot_general(left, right, (((1,), (1,)), ((), ())), preferred_element_type=F32)


def seen(shape, rows, y_index):
    n_y = shape[0] // rows
    key = lax.broadcasted_iota(jnp.int32, shape, 0)
    row = lax.broadcasted_iota(jnp.int32, shape, 1)
    ahead = key // rows
    block = lax.rem(y_index + ahead, n_y)
    return (block - y_index) * rows + key - ahead * rows <= row


def attend_kernel(
    place_ref, input_ref, up_ref, cos_ref, sin_ref, kv_ref, q_ref, o_ref, lse_ref,
    vt_ref, m_ref, l_ref, acc_ref,
):
    rows = input_ref.shape[0]
    chunk_rows = kv_ref.shape[0] // Z
    half = HD // 2

    @pl.when(pl.program_id(0) == 0)
    def _():
        for c in range(Z):
            at = slice(c * chunk_rows, (c + 1) * chunk_rows)
            vt_ref[:, at] = kv_ref[at, HD:].T

    cosine, sine = cos_ref[...], sin_ref[...]
    scale = 1.0 / math.sqrt(HD)
    raw = matmul(input_ref[...], up_ref[...])
    for j in range(STEP_HEADS):
        first, second = raw[:, j * HD : j * HD + half], raw[:, j * HD + half : (j + 1) * HD]
        turned = jnp.concatenate(
            [first * cosine - second * sine, second * cosine + first * sine], axis=1
        )
        q_ref[:, j * HD : (j + 1) * HD] = (turned.astype(BF).astype(F32) * scale).astype(BF)
    m_ref[...] = jnp.full_like(m_ref, NEG)
    l_ref[...] = jnp.zeros_like(l_ref)
    acc_ref[...] = jnp.zeros_like(acc_ref)

    def chunk(c, masked):
        at = pl.multiple_of(c * chunk_rows, chunk_rows)
        keys = kv_ref[pl.ds(at, chunk_rows), :HD]
        values = vt_ref[:, pl.ds(at, chunk_rows)]
        for j in range(STEP_HEADS):
            scores = dot_last(keys, q_ref[:, j * HD : (j + 1) * HD])
            if masked:
                scores = jnp.where(seen(scores.shape, rows, place_ref[1]), scores, NEG)
            peak = jnp.maximum(m_ref[j], jnp.max(scores, axis=0, keepdims=True))
            alpha = jnp.exp(m_ref[j] - peak)
            expo = jnp.exp(scores - peak)
            m_ref[j] = peak
            l_ref[j] = l_ref[j] * alpha + jnp.sum(expo, axis=0, keepdims=True)
            acc_ref[j] = acc_ref[j] * alpha + matmul(values, expo.astype(BF))

    @pl.loop(Z - place_ref[0], Z)
    def _(c):
        chunk(c, False)

    chunk(0, True)
    for j in range(STEP_HEADS):
        o_ref[:, j * HD : (j + 1) * HD] = (acc_ref[j] / l_ref[j]).T.astype(BF)
        lse_ref[j] = m_ref[j] + jnp.log(l_ref[j])


def attend(place, query_input, up_mat, cosine, sine, kv_whole):
    rows, rank = query_input.shape
    slot_len = kv_whole.shape[0]
    wide = STEP_HEADS * HD
    whole = lambda h, *_: (0, 0)
    by_head = lambda h, *_: (0, h)
    return pl.pallas_call(
        attend_kernel,
        out_shape=(
            jax.ShapeDtypeStruct((rows, HEADS * HD), BF),
            jax.ShapeDtypeStruct((rows, HEADS * HD), BF),
            jax.ShapeDtypeStruct((HEADS, 1, rows), F32),
        ),
        grid_spec=pltpu.PrefetchScalarGridSpec(
            num_scalar_prefetch=1,
            grid=(HEADS // STEP_HEADS,),
            in_specs=[
                pl.BlockSpec((rows, rank), whole),
                pl.BlockSpec((rank, wide), by_head),
                pl.BlockSpec((rows, HD // 2), whole),
                pl.BlockSpec((rows, HD // 2), whole),
                pl.BlockSpec((slot_len, 2 * HD), whole),
            ],
            out_specs=[
                pl.BlockSpec((rows, wide), by_head),
                pl.BlockSpec((rows, wide), by_head),
                pl.BlockSpec((STEP_HEADS, 1, rows), lambda h, *_: (h, 0, 0)),
            ],
            scratch_shapes=[
                pltpu.VMEM((HD, slot_len), BF),
                pltpu.VMEM((STEP_HEADS, 1, rows), F32),
                pltpu.VMEM((STEP_HEADS, 1, rows), F32),
                pltpu.VMEM((STEP_HEADS, HD, rows), F32),
            ],
        ),
        compiler_params=pltpu.CompilerParams(
            dimension_semantics=("arbitrary",), vmem_limit_bytes=40 * 1024 * 1024
        ),
        cost_estimate=pl.CostEstimate(
            flops=LIGHT, bytes_accessed=LIGHT, transcendentals=0
        ),
    )(place, query_input, up_mat, cosine, sine, kv_whole)


def attend_back_kernel(
    place_ref, q_ref, do_ref, o_ref, lse_ref, cos_ref, sin_ref, kv_ref, dq_ref, dkv_ref,
    acc_ref, dqs_ref,
):
    rows = q_ref.shape[0]
    chunk_rows = kv_ref.shape[0] // Z
    half = HD // 2
    step = pl.program_id(0)

    @pl.when(step == 0)
    def _():
        acc_ref[...] = jnp.zeros_like(acc_ref)

    dqs_ref[...] = jnp.zeros_like(dqs_ref)
    deltas = []
    for j in range(STEP_HEADS):
        at = slice(j * HD, (j + 1) * HD)
        prod = do_ref[:, at].astype(F32) * o_ref[:, at].astype(F32)
        deltas.append(jnp.sum(prod.T, axis=0, keepdims=True))

    def chunk(c, masked):
        at = pl.ds(pl.multiple_of(c * chunk_rows, chunk_rows), chunk_rows)
        keys = kv_ref[at, :HD]
        values = kv_ref[at, HD:]
        for j in range(STEP_HEADS):
            query = q_ref[:, j * HD : (j + 1) * HD]
            out_grad = do_ref[:, j * HD : (j + 1) * HD]
            probs = jnp.exp(dot_last(keys, query) - lse_ref[j])
            if masked:
                probs = jnp.where(seen(probs.shape, rows, place_ref[1]), probs, 0.0)
            score_grad = (probs * (dot_last(values, out_grad) - deltas[j])).astype(BF)
            acc_ref[at, HD:] += matmul(probs.astype(BF), out_grad)
            acc_ref[at, :HD] += matmul(score_grad, query)
            dqs_ref[j] += contract_rows(score_grad, keys)

    @pl.loop(Z - place_ref[0], Z)
    def _(c):
        chunk(c, False)

    chunk(0, True)
    cosine, sine = cos_ref[...], sin_ref[...]
    scale = 1.0 / math.sqrt(HD)
    for j in range(STEP_HEADS):
        first, second = dqs_ref[j, :, :half] * scale, dqs_ref[j, :, half:] * scale
        dq_ref[:, j * HD : (j + 1) * HD] = jnp.concatenate(
            [first * cosine + second * sine, second * cosine - first * sine], axis=1
        ).astype(BF)

    @pl.when(step == pl.num_programs(0) - 1)
    def _():
        dkv_ref[...] = acc_ref[...].astype(BF)


def attend_back(place, query, out_grad, attn_low, logsum, cosine, sine, kv_whole):
    rows = query.shape[0]
    slot_len = kv_whole.shape[0]
    wide = STEP_HEADS * HD
    whole = lambda h, *_: (0, 0)
    by_head = lambda h, *_: (0, h)
    return pl.pallas_call(
        attend_back_kernel,
        out_shape=(
            jax.ShapeDtypeStruct((rows, HEADS * HD), BF),
            jax.ShapeDtypeStruct((slot_len, 2 * HD), BF),
        ),
        grid_spec=pltpu.PrefetchScalarGridSpec(
            num_scalar_prefetch=1,
            grid=(HEADS // STEP_HEADS,),
            in_specs=[
                pl.BlockSpec((rows, wide), by_head),
                pl.BlockSpec((rows, wide), by_head),
                pl.BlockSpec((rows, wide), by_head),
                pl.BlockSpec((STEP_HEADS, 1, rows), lambda h, *_: (h, 0, 0)),
                pl.BlockSpec((rows, HD // 2), whole),
                pl.BlockSpec((rows, HD // 2), whole),
                pl.BlockSpec((slot_len, 2 * HD), whole),
            ],
            out_specs=[
                pl.BlockSpec((rows, wide), by_head),
                pl.BlockSpec((slot_len, 2 * HD), whole),
            ],
            scratch_shapes=[
                pltpu.VMEM((slot_len, 2 * HD), F32),
                pltpu.VMEM((STEP_HEADS, rows, HD), F32),
            ],
        ),
        compiler_params=pltpu.CompilerParams(
            dimension_semantics=("arbitrary",), vmem_limit_bytes=40 * 1024 * 1024
        ),
        cost_estimate=pl.CostEstimate(
            flops=LIGHT, bytes_accessed=LIGHT, transcendentals=0
        ),
    )(place, query, out_grad, attn_low, logsum, cosine, sine, kv_whole)


def interleave_kernel(n_shard, order_ref, gain_ref, weight_ref, *refs):
    *slot_refs, out_ref, sum_ref = refs
    n_group = len(slot_refs) // 2
    part = slot_refs[0].shape[1]
    unit = part // n_shard
    width = part * n_group
    total = 0.0
    gain = gain_ref[...]
    for half in range(2):
        slots = [ref[...].astype(F32) for ref in slot_refs[half * n_group : (half + 1) * n_group]]
        blocks = []
        for member in range(n_group):
            block = slots[0]
            for k in range(1, n_group):
                block = jnp.where(order_ref[member] == k, slots[k], block)
            blocks.append(block)
        row = jnp.concatenate(
            [
                blocks[member][:, s * unit : (s + 1) * unit]
                for s in range(n_shard)
                for member in range(n_group)
            ],
            axis=1,
        )
        at = slice(half * width, (half + 1) * width)
        total = total + jnp.sum(row * weight_ref[:, at].astype(F32), axis=1, keepdims=True)
        out_ref[:, at] = row * gain
    sum_ref[...] = total


def interleave(order, gain, weight, gate_slots, up_slots, n_shard):
    rows, width = weight.shape
    block = 32
    slots = [*gate_slots, *up_slots]
    by_row = lambda i, *_: (i, 0)
    return pl.pallas_call(
        lambda *refs: interleave_kernel(n_shard, *refs),
        out_shape=(
            jax.ShapeDtypeStruct((rows, width), F32),
            jax.ShapeDtypeStruct((rows, 1), F32),
        ),
        grid_spec=pltpu.PrefetchScalarGridSpec(
            num_scalar_prefetch=1,
            grid=(rows // block,),
            in_specs=[
                pl.BlockSpec((block, 1), by_row),
                pl.BlockSpec((block, width), by_row),
                *[pl.BlockSpec((block, slots[0].shape[1]), by_row) for _ in slots],
            ],
            out_specs=[
                pl.BlockSpec((block, width), by_row),
                pl.BlockSpec((block, 1), by_row),
            ],
        ),
        compiler_params=pltpu.CompilerParams(dimension_semantics=("arbitrary",)),
        cost_estimate=pl.CostEstimate(flops=LIGHT, bytes_accessed=LIGHT, transcendentals=0),
    )(order, gain, weight, *slots)


def select_kernel(n_shard, n_group, member_ref, gain_ref, weight_ref, gate_ref, up_ref):
    width = weight_ref.shape[1] // 2
    unit = width // n_shard // n_group
    gain = gain_ref[...]
    for half, out_ref in enumerate((gate_ref, up_ref)):
        pieces = []
        for s in range(n_shard):
            at = half * width + s * n_group * unit
            piece = weight_ref[:, at : at + unit].astype(F32)
            for k in range(1, n_group):
                other = weight_ref[:, at + k * unit : at + (k + 1) * unit].astype(F32)
                piece = jnp.where(member_ref[0] == k, other, piece)
            pieces.append(piece)
        out_ref[...] = (jnp.concatenate(pieces, axis=1) * gain).astype(BF)


def select_units(member, gain, weight, n_shard, n_group):
    rows, width = weight.shape
    block = 32
    part = width // 2 // n_group
    by_row = lambda i, *_: (i, 0)
    return pl.pallas_call(
        lambda *refs: select_kernel(n_shard, n_group, *refs),
        out_shape=(jax.ShapeDtypeStruct((rows, part), BF),) * 2,
        grid_spec=pltpu.PrefetchScalarGridSpec(
            num_scalar_prefetch=1,
            grid=(rows // block,),
            in_specs=[
                pl.BlockSpec((block, 1), by_row),
                pl.BlockSpec((block, width), by_row),
            ],
            out_specs=[pl.BlockSpec((block, part), by_row)] * 2,
        ),
        compiler_params=pltpu.CompilerParams(dimension_semantics=("arbitrary",)),
        cost_estimate=pl.CostEstimate(flops=LIGHT, bytes_accessed=LIGHT, transcendentals=0),
    )(member, gain, weight)


def from_ahead(value, axis, step):
    n = lax.axis_size(axis)
    return lax.ppermute(value, axis, [((j + step) % n, j) for j in range(n)])


def to_ahead(value, axis, step):
    n = lax.axis_size(axis)
    return lax.ppermute(value, axis, [(j, (j + step) % n) for j in range(n)])


def gather_group(value):
    n_x = lax.axis_size("x")
    mine = [value] + [from_ahead(value, "x", k) for k in range(1, n_x)]
    return mine + [from_ahead(v, "c", 1) for v in mine]


def reduce_group(parts):
    n_x = lax.axis_size("x")
    near, far = parts[:n_x], parts[n_x:]
    sums = [a + to_ahead(b.astype(BF), "c", 1).astype(F32) for a, b in zip(near, far)]
    total = sums[0]
    for k in range(1, n_x):
        total = total + to_ahead(sums[k].astype(BF), "x", k).astype(F32)
    return total


def exchange_group(value, pick):
    n_x = lax.axis_size("x")
    x_id, c_id = lax.axis_index("x"), lax.axis_index("c")
    out = []
    for dc in range(CORES):
        for dx in range(n_x):
            member = lax.rem(x_id + n_x - dx, n_x) * CORES + lax.rem(c_id + dc, CORES)
            block = pick(value, member)
            if dx or dc:
                perm = []
                for j in range(n_x):
                    for c in range(CORES):
                        source = ((j + dx) % n_x) * CORES + (c + dc) % CORES
                        perm.append((source, j * CORES + c))
                block = lax.ppermute(block, ("x", "c"), perm)
            out.append(block)
    return out


def shard_offsets():
    return [(dz, dy) for dz in range(Z) for dy in range(lax.axis_size("y"))]


def shard_permute(value, dz, dy, ahead):
    n_y = lax.axis_size("y")
    perm = []
    for z in range(Z):
        for y in range(n_y):
            far, near = ((z + dz) % Z) * n_y + (y + dy) % n_y, z * n_y + y
            perm.append((near, far) if ahead else (far, near))
    return lax.ppermute(value, ("z", "y"), perm)


def position_of(dz, dy):
    n_y = lax.axis_size("y")
    return lax.rem(lax.axis_index("z") + dz, Z) * n_y + lax.rem(lax.axis_index("y") + dy, n_y)


def ring_z(value):
    return [from_ahead(value, "z", k) if k else value for k in range(Z)]


def small_over_y(blocks):
    total = jnp.stack(blocks[0]).astype(F32)
    for k, group in enumerate(blocks[1:]):
        total = total + to_ahead(jnp.stack(group).astype(BF), "y", k + 1).astype(F32)
    return total


def small_over_z(total):
    low = total.astype(BF)
    return [total[0]] + [to_ahead(low[k], "z", k) for k in range(1, Z)]


def added(blocks):
    total = blocks[0]
    for block in blocks[1:]:
        total = total + block.astype(F32)
    return total


def after(values, done):
    return lax.optimization_barrier((values, done))[0]


def gather_z(value):
    return lax.all_gather(value, "z", axis=0, tiled=True)


def gather_shard(value):
    return lax.all_gather(value, ("z", "y"), axis=0, tiled=True)


def scatter_z(value):
    return lax.psum_scatter(value, "z", scatter_dimension=0, tiled=True)


def begin_reduce_y(value):
    n_y = lax.axis_size("y")
    index = lax.axis_index("y")
    blocks = value.astype(BF).reshape(Z, n_y, -1, value.shape[1])
    own = lax.dynamic_index_in_dim(blocks, index, axis=1, keepdims=False)
    others = []
    for k in range(1, n_y):
        block = lax.dynamic_index_in_dim(blocks, lax.rem(index + k, n_y), axis=1, keepdims=False)
        others.append(to_ahead(block, "y", k))
    return own, others


def end_reduce_y(own, others):
    total = own.astype(F32)
    for block in others:
        total = total + block.astype(F32)
    return total.astype(BF).reshape(-1, own.shape[-1])


def swap_y(wide):
    n_y = lax.axis_size("y")
    return [wide] + [from_ahead(wide, "y", k) for k in range(1, n_y)]


def merge_y(blocks, n):
    n_y = lax.axis_size("y")
    m = blocks[0].shape[1]
    blocks = [block.reshape(Z, 1, n, m) for block in blocks]
    if n_y == 2:
        first, second = blocks
        return jnp.where(
            lax.axis_index("y") == 0,
            jnp.concatenate([first, second], axis=1),
            jnp.concatenate([second, first], axis=1),
        ).reshape(-1, m)
    at = lax.rem(n_y - lax.axis_index("y"), n_y)
    stacked = jnp.concatenate(blocks + blocks[:-1], axis=1)
    return lax.dynamic_slice_in_dim(stacked, at, n_y, axis=1).reshape(-1, m)


def merge_own_y(blocks):
    n_y = lax.axis_size("y")
    if n_y == 2:
        first, second = blocks
        return jnp.where(
            lax.axis_index("y") == 0,
            jnp.concatenate([first, second]),
            jnp.concatenate([second, first]),
        )
    n = blocks[0].shape[0]
    at = lax.rem(n_y - lax.axis_index("y"), n_y) * n
    return lax.dynamic_slice_in_dim(jnp.concatenate(blocks + blocks[:-1]), at, n_y * n)


def reduce_own_y(value):
    n_y = lax.axis_size("y")
    index = lax.axis_index("y")
    blocks = value.reshape(n_y, -1, value.shape[1])
    total = lax.dynamic_index_in_dim(blocks, index, keepdims=False).astype(F32)
    for k in range(1, n_y):
        other = lax.dynamic_index_in_dim(blocks, lax.rem(index + k, n_y), keepdims=False)
        total = total + to_ahead(other, "y", k).astype(F32)
    return total.astype(BF)


def member_of(dc, dx):
    n_x = lax.axis_size("x")
    x_id = lax.rem(lax.axis_index("x") + dx, n_x)
    return x_id * CORES + lax.rem(lax.axis_index("c") + dc, CORES)


def offsets():
    return [(dc, dx) for dc in range(CORES) for dx in range(lax.axis_size("x"))]


def place_group(slots, axis, dtype):
    n = slots[0].shape[axis]
    shape = list(slots[0].shape)
    shape[axis] = n * len(slots)
    out = jnp.zeros(shape, dtype)
    for (dc, dx), slot in zip(offsets(), slots):
        start = [0] * len(shape)
        start[axis] = member_of(dc, dx) * n
        out = lax.dynamic_update_slice(out, slot.astype(dtype), start)
    return out


def spread_begin(wide):
    n_y, n_x = lax.axis_size("y"), lax.axis_size("x")
    over_y = [wide] + [from_ahead(wide, "y", k) for k in range(1, n_y)]
    over_x = [from_ahead(wide, "x", k) for k in range(1, n_x)]
    return over_y, over_x


def spread_next(over_y, over_x):
    n_x = lax.axis_size("x")
    return [[over_y[0]] + over_x] + [
        [block] + [from_ahead(block, "x", k) for k in range(1, n_x)] for block in over_y[1:]
    ]


def spread_end(grid):
    return [group + [from_ahead(block, "c", 1) for block in group] for group in grid]


def place_every(slots, n):
    n_y, n_x = lax.axis_size("y"), lax.axis_size("x")
    m = slots[0][0].shape[1]
    out = jnp.zeros((Z, n_y, n_x * CORES, n, m), BF)
    for ky, group in enumerate(slots):
        at_y = lax.rem(lax.axis_index("y") + ky, n_y)
        for (dc, dx), slot in zip(offsets(), group):
            out = lax.dynamic_update_slice(
                out, slot.reshape(Z, 1, 1, n, m), (0, at_y, member_of(dc, dx), 0, 0)
            )
    return out.reshape(-1, m)


def on_device(
    tokens,
    cotangent,
    lengths,
    attn_gain,
    query_down,
    key_value,
    query_gain,
    query_up,
    out_proj,
    mlp_gain,
    gate_up,
    down_proj,
):
    n_x = lax.axis_size("x")
    n_group = n_x * CORES
    n_y = lax.axis_size("y")
    n_shard = Z * n_y
    _, rows, width = tokens.shape
    rank = query_down.shape[1]
    group_id = lax.axis_index("x") * CORES + lax.axis_index("c")
    shard_id = lax.axis_index("z") * n_y + lax.axis_index("y")

    def quarter_rows(value):
        n = value.shape[0] // n_group
        return lax.dynamic_slice_in_dim(value, group_id * n, n, axis=0)

    def pick_cols(value, member):
        n = value.shape[1] // n_group
        return lax.dynamic_slice_in_dim(value, member * n, n, axis=1)

    def scaled(weight, gain):
        return (weight.astype(F32) * gain.astype(F32)[:, None]).astype(BF)

    def split(value):
        return [value[k * rows : (k + 1) * rows] for k in range(n_group)]

    qkv_own = jnp.concatenate([query_down, key_value], axis=1)
    qkv_ring = ring_z(scaled(pick_cols(qkv_own, group_id), attn_gain))
    qup_own = quarter_rows(scaled(query_up, query_gain))
    qup_mat = lax.all_gather(qup_own, ("z", "y", "x", "c"), axis=0, tiled=True)
    out_wide = gather_z(quarter_rows(out_proj))

    my_length = lax.dynamic_index_in_dim(lengths, group_id, keepdims=False)
    positions = shard_id * rows + jnp.arange(rows, dtype=jnp.int32)
    place = jnp.stack([lax.axis_index("z"), lax.axis_index("y")]).astype(jnp.int32)
    valid = (positions < my_length).astype(F32)[:, None]
    cosine, sine = rope_tables(positions, HD)

    x_rows = tokens[0].astype(F32)
    rms_first = inv_rms(x_rows)
    normed_first = x_rows * rms_first
    attn_input = normed_first.astype(BF)
    input_all = jnp.concatenate(gather_group(attn_input), axis=0)

    qkv_stack = jnp.stack(qkv_ring)
    qkv_grid = [qkv_stack] + [from_ahead(qkv_stack, "y", k) for k in range(1, n_y)]

    gate_up_late = after(gate_up, qkv_ring[1])
    gate_own, up_own = select_units(
        group_id.astype(jnp.int32).reshape(1),
        mlp_gain.astype(F32)[:, None],
        gate_up_late,
        n_shard,
        n_group,
    )
    gate_wide = gather_z(gate_own)

    qkv_mat = jnp.zeros((width, qkv_stack.shape[2]), BF)
    for dy, stack in enumerate(qkv_grid):
        for dz in range(Z):
            at = position_of(dz, dy) * stack.shape[1]
            qkv_mat = lax.dynamic_update_slice(qkv_mat, stack[dz], (at, 0))
    qkv_flat = matmul(input_all, qkv_mat)
    up_wide = gather_z(up_own)
    blocks = []
    for (dc, dx), block in zip(offsets(), split(qkv_flat)):
        if dc or dx:
            perm = []
            for j in range(n_x):
                for c in range(CORES):
                    target = ((j + dx) % n_x) * CORES + (c + dc) % CORES
                    perm.append((j * CORES + c, target))
            block = lax.ppermute(block, ("x", "c"), perm)
        blocks.append(block)
    qkv_out = jnp.zeros((rows, qkv_own.shape[1]), F32)
    n_cols = qkv_own.shape[1] // n_group
    for (dc, dx), block in zip(offsets(), blocks):
        member = lax.rem(lax.axis_index("x") + n_x - dx, n_x) * CORES
        member = member + lax.rem(lax.axis_index("c") + dc, CORES)
        qkv_out = lax.dynamic_update_slice(qkv_out, block, (0, member * n_cols))
    qdown_out, kv_out = qkv_out[:, :rank], qkv_out[:, rank:]

    key_rot = rotate(kv_out[:, :HD], cosine, sine).astype(BF)
    kv_local = jnp.concatenate([key_rot, kv_out[:, HD:].astype(BF)], axis=1)
    out_first = spread_begin(out_wide)
    kv_local = after(kv_local, out_wide)
    kv_ring = ring_z(kv_local)
    down_both = [quarter_rows(down_proj)]
    down_both += [from_ahead(after(down_both[0], qkv_flat), "y", k) for k in range(1, n_y)]
    down_mat = gather_z(merge_own_y(down_both))
    rms_query = inv_rms(qdown_out)
    normed_query = qdown_out * rms_query
    query_input = normed_query.astype(BF)
    kv_stack = jnp.stack(kv_ring)
    kv_grid = [kv_stack] + [from_ahead(kv_stack, "y", k) for k in range(1, n_y)]
    kv_grid = after(kv_grid, out_first)
    kv_whole = jnp.concatenate([stack[dz] for dz in range(Z) for stack in kv_grid])
    out_grid = spread_next(*out_first)
    query_rot, attn_low, logsum = attend(place, query_input, qup_mat, cosine, sine, kv_whole)
    gate_blocks = swap_y(gate_wide)
    out_slots = spread_end(after(out_grid, attn_low))
    out_mat = place_every(out_slots, out_proj.shape[0] // n_group)
    middle = x_rows + matmul(attn_low, out_mat)
    rms_second = inv_rms(middle)
    normed_second = middle * rms_second
    mlp_input = normed_second.astype(BF)

    mlp_all = jnp.concatenate(gather_group(mlp_input), axis=0)
    up_blocks = swap_y(up_wide)
    cot_rows = cotangent[0].astype(F32) * valid
    cot_late = after(cot_rows.astype(BF), mlp_input)
    cot_all = jnp.concatenate(gather_group(cot_late), axis=0)
    gate_mat = merge_y(after(gate_blocks, mlp_all), mlp_gain.shape[0])
    gate_part = matmul(mlp_all, gate_mat)
    up_mat = merge_y(after(up_blocks, (gate_part, down_mat)), mlp_gain.shape[0])
    def pick_out(value, member):
        parts = value.reshape(rows, n_shard, n_group, -1)
        return lax.dynamic_index_in_dim(parts, member, axis=2, keepdims=False).reshape(rows, -1)

    attn_late, query_late = after((attn_low, query_input), mlp_all)
    attn_all = jnp.concatenate(exchange_group(attn_late, pick_out), axis=0)
    query_all = jnp.concatenate(gather_group(query_late), axis=0)

    up_mat, attn_all, query_all = lax.optimization_barrier((up_mat, attn_all, query_all))
    up_part = matmul(mlp_all, up_mat)
    sigmoid_gate = jax.nn.sigmoid(gate_part)
    activated = gate_part * sigmoid_gate
    hidden_low = (activated * up_part).astype(BF)

    down_term = contract_rows(hidden_low, cot_all).astype(BF)
    down_half = scatter_z(down_term)
    down_mat = after(down_mat, down_term)
    hidden_grad = contract_cols(cot_all, down_mat)
    gate_grad = hidden_grad * up_part * (sigmoid_gate * (1.0 + gate_part * (1.0 - sigmoid_gate)))
    gate_low = gate_grad.astype(BF)
    up_low = (hidden_grad * activated).astype(BF)
    partial_in = contract_cols(gate_low, gate_mat) + contract_cols(up_low, up_mat)
    gate_low, up_low = after((gate_low, up_low), partial_in)
    gate_term = contract_rows(mlp_all, gate_low).astype(BF)
    gate_ends = begin_reduce_y(gate_term)
    up_term = contract_rows(mlp_all, after(up_low, gate_term)).astype(BF)
    up_half = scatter_z(up_term)
    mlp_in_grad = after(reduce_group(split(partial_in)), up_term)

    middle_grad = cot_rows + rms_second * (
        mlp_in_grad
        - normed_second * jnp.mean(mlp_in_grad * normed_second, axis=-1, keepdims=True)
    )
    middle_low = middle_grad.astype(BF)
    middle_all = jnp.concatenate(gather_group(middle_low), axis=0)
    attn_val_grad = contract_cols(middle_low, out_mat).astype(BF)
    query_raw_grad, kv_term = attend_back(
        place, query_rot, attn_val_grad, attn_low, logsum, cosine, sine, kv_whole
    )
    kv_slots = [kv_term[k * rows : (k + 1) * rows] for k in range(Z * n_y)]
    kv_near = small_over_y([kv_slots[k::n_y] for k in range(n_y)])
    kv_blocks = small_over_z(kv_near)
    gate_pre = end_reduce_y(gate_ends[0], after(gate_ends[1], kv_term))
    gate_sum = scatter_z(gate_pre)
    out_term = contract_rows(attn_all, after(middle_all, gate_pre)).astype(BF)
    out_ends = begin_reduce_y(out_term)
    kv_blocks, out_term = lax.optimization_barrier((kv_blocks, out_term))
    kv_grad = added(kv_blocks)
    raw_all = jnp.concatenate(exchange_group(query_raw_grad, pick_cols), axis=0)
    query_in_grad = contract_cols(query_raw_grad, qup_mat)
    qup_term = contract_rows(query_all, raw_all).astype(BF)
    qdown_grad = rms_query * (
        query_in_grad
        - normed_query * jnp.mean(query_in_grad * normed_query, axis=-1, keepdims=True)
    )
    kv_grad, qup_term = lax.optimization_barrier((kv_grad, qup_term))
    key_raw_grad = rotate_back(kv_grad[:, :HD], cosine, sine)
    qkv_low = jnp.concatenate([qdown_grad, key_raw_grad, kv_grad[:, HD:]], axis=1).astype(BF)
    qkv_parts, out_ends = lax.optimization_barrier(
        (exchange_group(qkv_low, pick_cols), out_ends)
    )
    out_pre = end_reduce_y(*out_ends)
    out_sum = scatter_z(out_pre)
    qkv_all = jnp.concatenate(after(qkv_parts, out_pre), axis=0)
    qkv_term = contract_rows(input_all, qkv_all).astype(BF)
    n_own = query_down.shape[0]
    qkv_near = small_over_y(
        [
            [
                lax.dynamic_slice_in_dim(qkv_term, position_of(dz, dy) * n_own, n_own)
                for dz in range(Z)
            ]
            for dy in range(n_y)
        ]
    )
    first_part = contract_cols(after(qkv_all, qkv_term), qkv_mat)
    first_in_grad = reduce_group(split(first_part))
    qup_ends = begin_reduce_y(after(qup_term, out_ends))
    layer_part = matmul(after(hidden_low, first_part), down_mat)
    down_sum = reduce_own_y(after(down_half, layer_part))
    up_sum = reduce_own_y(after(up_half, down_half))
    qup_ends, first_in_grad, layer_part, up_sum = lax.optimization_barrier(
        (qup_ends, first_in_grad, layer_part, up_sum)
    )
    qup_pre = end_reduce_y(*qup_ends)
    qup_sum = scatter_z(qup_pre)
    layer_sum = reduce_group(split(layer_part))
    up_slots = gather_group(up_sum)
    gate_slots = gather_group(after(gate_sum, up_sum))
    down_slots = gather_group(down_sum)
    qkv_blocks = small_over_z(qkv_near)
    qkv_blocks, up_slots, gate_slots = lax.optimization_barrier(
        (qkv_blocks, up_slots, gate_slots)
    )
    input_rows_grad = middle_grad + rms_first * (
        first_in_grad
        - normed_first * jnp.mean(first_in_grad * normed_first, axis=-1, keepdims=True)
    )
    order = jnp.zeros((n_group,), jnp.int32)
    for k, (dc, dx) in enumerate(offsets()):
        order = order.at[member_of(dc, dx)].set(k)
    gateup_grad, second_gain_grad = interleave(
        order, mlp_gain.astype(F32)[:, None], gate_up, gate_slots, up_slots, n_shard
    )
    qkv_blocks, gateup_grad, layer_sum, down_slots = lax.optimization_barrier(
        (qkv_blocks, gateup_grad, layer_sum, down_slots)
    )
    qkv_sum = added(qkv_blocks).astype(BF)
    layer = (middle + layer_sum) * valid
    out_slots = gather_group(after(out_sum, gate_slots))

    down_grad = place_group(down_slots, 0, F32)
    out_grad = place_group(out_slots, 0, F32)
    qup_raw = place_group(gather_group(after(qup_sum, out_slots)), 1, F32)
    qkv_raw = place_group(gather_group(qkv_sum), 1, F32)

    def gain_grad(weight, grad):
        return jnp.sum(weight.astype(F32) * grad, axis=1)

    qkv_weight_grad = qkv_raw * attn_gain.astype(F32)[:, None]
    return (
        layer.astype(BF)[None],
        input_rows_grad.astype(BF)[None],
        gain_grad(qkv_own, qkv_raw),
        qkv_weight_grad[:, :rank],
        qkv_weight_grad[:, rank:],
        gain_grad(query_up, qup_raw),
        qup_raw * query_gain.astype(F32)[:, None],
        out_grad,
        second_gain_grad[:, 0],
        gateup_grad,
        down_grad,
    )


def solution(mesh):
    n_replica, n_shard = mesh.devices.shape
    devices = mesh.devices.reshape(n_replica // CORES, CORES, Z, n_shard // Z)
    inner = Mesh(devices, ("x", "c", "z", "y"))
    group, shard = ("x", "c"), ("z", "y")
    acts = P(group, shard, None)
    vec = P(shard)
    mat = P(shard, None)
    in_specs = (acts, acts, P(), vec, mat, mat, vec, mat, mat, vec, mat, mat)
    out_specs = (acts, acts, vec, mat, mat, vec, mat, mat, vec, mat, mat)
    return jax.shard_map(
        on_device, mesh=inner, in_specs=in_specs, out_specs=out_specs, check_vma=False
    )
```

```python
import math

import jax
import jax.numpy as jnp
from jax import lax
from jax.experimental import pallas as pl
from jax.experimental.pallas import tpu as pltpu
from jax.sharding import Mesh
from jax.sharding import PartitionSpec as P

HEADS = 16
HD = 256
FF = 5632
Z = 4
CORES = 2


EPSILON = 1e-06
BF = jnp.bfloat16
F32 = jnp.float32


def inv_rms(values):
    return lax.rsqrt(jnp.mean(values * values, axis=-1, keepdims=True) + EPSILON)


def rope_tables(positions, head_dim):
    half_dim = head_dim // 2
    frequency = jnp.exp(-math.log(10000.0) * jnp.arange(half_dim).astype(F32) / half_dim)
    angles = positions.astype(F32)[:, None] * frequency[None, :]
    return (jnp.cos(angles), jnp.sin(angles))


def rotate(values, cosine, sine):
    half_dim = values.shape[-1] // 2
    first_half = values[..., :half_dim]
    second_half = values[..., half_dim:]
    return jnp.concatenate(
        [first_half * cosine - second_half * sine, second_half * cosine + first_half * sine],
        axis=-1,
    )


def rotate_back(grads, cosine, sine):
    half_dim = grads.shape[-1] // 2
    first_half = grads[..., :half_dim]
    second_half = grads[..., half_dim:]
    return jnp.concatenate(
        [first_half * cosine + second_half * sine, second_half * cosine - first_half * sine],
        axis=-1,
    )


def matmul(left, right):
    return jnp.dot(left, right, preferred_element_type=F32)


def contract_rows(left, right):
    return lax.dot_general(left, right, (((0,), (0,)), ((), ())), preferred_element_type=F32)


def contract_cols(left, right):
    return lax.dot_general(left, right, (((1,), (1,)), ((), ())), preferred_element_type=F32)


STEP_HEADS = 2
LIGHT = 1000
NEG = -1e30


def dot_last(left, right):
    return lax.dot_general(left, right, (((1,), (1,)), ((), ())), preferred_element_type=F32)


def seen(shape, rows, y_index):
    n_y = shape[0] // rows
    key = lax.broadcasted_iota(jnp.int32, shape, 0)
    row = lax.broadcasted_iota(jnp.int32, shape, 1)
    ahead = key // rows
    block = lax.rem(y_index + ahead, n_y)
    return (block - y_index) * rows + key - ahead * rows <= row


def attend_kernel(
    place_ref, input_ref, up_ref, cos_ref, sin_ref, kv_ref, q_ref, o_ref, lse_ref,
    vt_ref, m_ref, l_ref, acc_ref,
):
    rows = input_ref.shape[0]
    chunk_rows = kv_ref.shape[0] // Z
    half = HD // 2

    @pl.when(pl.program_id(0) == 0)
    def _():
        for c in range(Z):
            at = slice(c * chunk_rows, (c + 1) * chunk_rows)
            vt_ref[:, at] = kv_ref[at, HD:].T

    cosine, sine = cos_ref[...], sin_ref[...]
    scale = 1.0 / math.sqrt(HD)
    raw = matmul(input_ref[...], up_ref[...])
    for j in range(STEP_HEADS):
        first, second = raw[:, j * HD : j * HD + half], raw[:, j * HD + half : (j + 1) * HD]
        turned = jnp.concatenate(
            [first * cosine - second * sine, second * cosine + first * sine], axis=1
        )
        q_ref[:, j * HD : (j + 1) * HD] = (turned.astype(BF).astype(F32) * scale).astype(BF)
    m_ref[...] = jnp.full_like(m_ref, NEG)
    l_ref[...] = jnp.zeros_like(l_ref)
    acc_ref[...] = jnp.zeros_like(acc_ref)

    def chunk(c, masked):
        at = pl.multiple_of(c * chunk_rows, chunk_rows)
        keys = kv_ref[pl.ds(at, chunk_rows), :HD]
        values = vt_ref[:, pl.ds(at, chunk_rows)]
        for j in range(STEP_HEADS):
            scores = dot_last(keys, q_ref[:, j * HD : (j + 1) * HD])
            if masked:
                scores = jnp.where(seen(scores.shape, rows, place_ref[1]), scores, NEG)
            peak = jnp.maximum(m_ref[j], jnp.max(scores, axis=0, keepdims=True))
            alpha = jnp.exp(m_ref[j] - peak)
            expo = jnp.exp(scores - peak)
            m_ref[j] = peak
            l_ref[j] = l_ref[j] * alpha + jnp.sum(expo, axis=0, keepdims=True)
            acc_ref[j] = acc_ref[j] * alpha + matmul(values, expo.astype(BF))

    @pl.loop(Z - place_ref[0], Z)
    def _(c):
        chunk(c, False)

    chunk(0, True)
    for j in range(STEP_HEADS):
        o_ref[:, j * HD : (j + 1) * HD] = (acc_ref[j] / l_ref[j]).T.astype(BF)
        lse_ref[j] = m_ref[j] + jnp.log(l_ref[j])


def attend(place, query_input, up_mat, cosine, sine, kv_whole):
    rows, rank = query_input.shape
    slot_len = kv_whole.shape[0]
    wide = STEP_HEADS * HD
    whole = lambda h, *_: (0, 0)
    by_head = lambda h, *_: (0, h)
    return pl.pallas_call(
        attend_kernel,
        out_shape=(
            jax.ShapeDtypeStruct((rows, HEADS * HD), BF),
            jax.ShapeDtypeStruct((rows, HEADS * HD), BF),
            jax.ShapeDtypeStruct((HEADS, 1, rows), F32),
        ),
        grid_spec=pltpu.PrefetchScalarGridSpec(
            num_scalar_prefetch=1,
            grid=(HEADS // STEP_HEADS,),
            in_specs=[
                pl.BlockSpec((rows, rank), whole),
                pl.BlockSpec((rank, wide), by_head),
                pl.BlockSpec((rows, HD // 2), whole),
                pl.BlockSpec((rows, HD // 2), whole),
                pl.BlockSpec((slot_len, 2 * HD), whole),
            ],
            out_specs=[
                pl.BlockSpec((rows, wide), by_head),
                pl.BlockSpec((rows, wide), by_head),
                pl.BlockSpec((STEP_HEADS, 1, rows), lambda h, *_: (h, 0, 0)),
            ],
            scratch_shapes=[
                pltpu.VMEM((HD, slot_len), BF),
                pltpu.VMEM((STEP_HEADS, 1, rows), F32),
                pltpu.VMEM((STEP_HEADS, 1, rows), F32),
                pltpu.VMEM((STEP_HEADS, HD, rows), F32),
            ],
        ),
        compiler_params=pltpu.CompilerParams(
            dimension_semantics=("arbitrary",), vmem_limit_bytes=40 * 1024 * 1024
        ),
        cost_estimate=pl.CostEstimate(
            flops=LIGHT, bytes_accessed=LIGHT, transcendentals=0
        ),
    )(place, query_input, up_mat, cosine, sine, kv_whole)


def attend_back_kernel(
    place_ref, q_ref, do_ref, o_ref, lse_ref, cos_ref, sin_ref, kv_ref, dq_ref, dkv_ref,
    acc_ref, dqs_ref,
):
    rows = q_ref.shape[0]
    chunk_rows = kv_ref.shape[0] // Z
    half = HD // 2
    step = pl.program_id(0)

    @pl.when(step == 0)
    def _():
        acc_ref[...] = jnp.zeros_like(acc_ref)

    dqs_ref[...] = jnp.zeros_like(dqs_ref)
    deltas = []
    for j in range(STEP_HEADS):
        at = slice(j * HD, (j + 1) * HD)
        prod = do_ref[:, at].astype(F32) * o_ref[:, at].astype(F32)
        deltas.append(jnp.sum(prod.T, axis=0, keepdims=True))

    def chunk(c, masked):
        at = pl.ds(pl.multiple_of(c * chunk_rows, chunk_rows), chunk_rows)
        keys = kv_ref[at, :HD]
        values = kv_ref[at, HD:]
        for j in range(STEP_HEADS):
            query = q_ref[:, j * HD : (j + 1) * HD]
            out_grad = do_ref[:, j * HD : (j + 1) * HD]
            probs = jnp.exp(dot_last(keys, query) - lse_ref[j])
            if masked:
                probs = jnp.where(seen(probs.shape, rows, place_ref[1]), probs, 0.0)
            score_grad = (probs * (dot_last(values, out_grad) - deltas[j])).astype(BF)
            acc_ref[at, HD:] += matmul(probs.astype(BF), out_grad)
            acc_ref[at, :HD] += matmul(score_grad, query)
            dqs_ref[j] += contract_rows(score_grad, keys)

    @pl.loop(Z - place_ref[0], Z)
    def _(c):
        chunk(c, False)

    chunk(0, True)
    cosine, sine = cos_ref[...], sin_ref[...]
    scale = 1.0 / math.sqrt(HD)
    for j in range(STEP_HEADS):
        first, second = dqs_ref[j, :, :half] * scale, dqs_ref[j, :, half:] * scale
        dq_ref[:, j * HD : (j + 1) * HD] = jnp.concatenate(
            [first * cosine + second * sine, second * cosine - first * sine], axis=1
        ).astype(BF)

    @pl.when(step == pl.num_programs(0) - 1)
    def _():
        dkv_ref[...] = acc_ref[...].astype(BF)


def attend_back(place, query, out_grad, attn_low, logsum, cosine, sine, kv_whole):
    rows = query.shape[0]
    slot_len = kv_whole.shape[0]
    wide = STEP_HEADS * HD
    whole = lambda h, *_: (0, 0)
    by_head = lambda h, *_: (0, h)
    return pl.pallas_call(
        attend_back_kernel,
        out_shape=(
            jax.ShapeDtypeStruct((rows, HEADS * HD), BF),
            jax.ShapeDtypeStruct((slot_len, 2 * HD), BF),
        ),
        grid_spec=pltpu.PrefetchScalarGridSpec(
            num_scalar_prefetch=1,
            grid=(HEADS // STEP_HEADS,),
            in_specs=[
                pl.BlockSpec((rows, wide), by_head),
                pl.BlockSpec((rows, wide), by_head),
                pl.BlockSpec((rows, wide), by_head),
                pl.BlockSpec((STEP_HEADS, 1, rows), lambda h, *_: (h, 0, 0)),
                pl.BlockSpec((rows, HD // 2), whole),
                pl.BlockSpec((rows, HD // 2), whole),
                pl.BlockSpec((slot_len, 2 * HD), whole),
            ],
            out_specs=[
                pl.BlockSpec((rows, wide), by_head),
                pl.BlockSpec((slot_len, 2 * HD), whole),
            ],
            scratch_shapes=[
                pltpu.VMEM((slot_len, 2 * HD), F32),
                pltpu.VMEM((STEP_HEADS, rows, HD), F32),
            ],
        ),
        compiler_params=pltpu.CompilerParams(
            dimension_semantics=("arbitrary",), vmem_limit_bytes=40 * 1024 * 1024
        ),
        cost_estimate=pl.CostEstimate(
            flops=LIGHT, bytes_accessed=LIGHT, transcendentals=0
        ),
    )(place, query, out_grad, attn_low, logsum, cosine, sine, kv_whole)


def interleave_kernel(n_shard, order_ref, gain_ref, weight_ref, *refs):
    *slot_refs, out_ref, sum_ref = refs
    n_group = len(slot_refs) // 2
    part = slot_refs[0].shape[1]
    unit = part // n_shard
    width = part * n_group
    total = 0.0
    gain = gain_ref[...]
    for half in range(2):
        slots = [ref[...].astype(F32) for ref in slot_refs[half * n_group : (half + 1) * n_group]]
        blocks = []
        for member in range(n_group):
            block = slots[0]
            for k in range(1, n_group):
                block = jnp.where(order_ref[member] == k, slots[k], block)
            blocks.append(block)
        row = jnp.concatenate(
            [
                blocks[member][:, s * unit : (s + 1) * unit]
                for s in range(n_shard)
                for member in range(n_group)
            ],
            axis=1,
        )
        at = slice(half * width, (half + 1) * width)
        total = total + jnp.sum(row * weight_ref[:, at].astype(F32), axis=1, keepdims=True)
        out_ref[:, at] = row * gain
    sum_ref[...] = total


def interleave(order, gain, weight, gate_slots, up_slots, n_shard):
    rows, width = weight.shape
    block = 32
    slots = [*gate_slots, *up_slots]
    by_row = lambda i, *_: (i, 0)
    return pl.pallas_call(
        lambda *refs: interleave_kernel(n_shard, *refs),
        out_shape=(
            jax.ShapeDtypeStruct((rows, width), F32),
            jax.ShapeDtypeStruct((rows, 1), F32),
        ),
        grid_spec=pltpu.PrefetchScalarGridSpec(
            num_scalar_prefetch=1,
            grid=(rows // block,),
            in_specs=[
                pl.BlockSpec((block, 1), by_row),
                pl.BlockSpec((block, width), by_row),
                *[pl.BlockSpec((block, slots[0].shape[1]), by_row) for _ in slots],
            ],
            out_specs=[
                pl.BlockSpec((block, width), by_row),
                pl.BlockSpec((block, 1), by_row),
            ],
        ),
        compiler_params=pltpu.CompilerParams(dimension_semantics=("arbitrary",)),
        cost_estimate=pl.CostEstimate(flops=LIGHT, bytes_accessed=LIGHT, transcendentals=0),
    )(order, gain, weight, *slots)


def select_kernel(n_shard, n_group, member_ref, gain_ref, weight_ref, gate_ref, up_ref):
    width = weight_ref.shape[1] // 2
    unit = width // n_shard // n_group
    gain = gain_ref[...]
    for half, out_ref in enumerate((gate_ref, up_ref)):
        pieces = []
        for s in range(n_shard):
            at = half * width + s * n_group * unit
            piece = weight_ref[:, at : at + unit].astype(F32)
            for k in range(1, n_group):
                other = weight_ref[:, at + k * unit : at + (k + 1) * unit].astype(F32)
                piece = jnp.where(member_ref[0] == k, other, piece)
            pieces.append(piece)
        out_ref[...] = (jnp.concatenate(pieces, axis=1) * gain).astype(BF)


def select_units(member, gain, weight, n_shard, n_group):
    rows, width = weight.shape
    block = 32
    part = width // 2 // n_group
    by_row = lambda i, *_: (i, 0)
    return pl.pallas_call(
        lambda *refs: select_kernel(n_shard, n_group, *refs),
        out_shape=(jax.ShapeDtypeStruct((rows, part), BF),) * 2,
        grid_spec=pltpu.PrefetchScalarGridSpec(
            num_scalar_prefetch=1,
            grid=(rows // block,),
            in_specs=[
                pl.BlockSpec((block, 1), by_row),
                pl.BlockSpec((block, width), by_row),
            ],
            out_specs=[pl.BlockSpec((block, part), by_row)] * 2,
        ),
        compiler_params=pltpu.CompilerParams(dimension_semantics=("arbitrary",)),
        cost_estimate=pl.CostEstimate(flops=LIGHT, bytes_accessed=LIGHT, transcendentals=0),
    )(member, gain, weight)


def from_ahead(value, axis, step):
    n = lax.axis_size(axis)
    return lax.ppermute(value, axis, [((j + step) % n, j) for j in range(n)])


def to_ahead(value, axis, step):
    n = lax.axis_size(axis)
    return lax.ppermute(value, axis, [(j, (j + step) % n) for j in range(n)])


def gather_group(value):
    n_x = lax.axis_size("x")
    mine = [value] + [from_ahead(value, "x", k) for k in range(1, n_x)]
    return mine + [from_ahead(v, "c", 1) for v in mine]


def reduce_group(parts):
    n_x = lax.axis_size("x")
    near, far = parts[:n_x], parts[n_x:]
    sums = [a + to_ahead(b.astype(BF), "c", 1).astype(F32) for a, b in zip(near, far)]
    total = sums[0]
    for k in range(1, n_x):
        total = total + to_ahead(sums[k].astype(BF), "x", k).astype(F32)
    return total


def exchange_group(value, pick):
    n_x = lax.axis_size("x")
    x_id, c_id = lax.axis_index("x"), lax.axis_index("c")
    out = []
    for dc in range(CORES):
        for dx in range(n_x):
            member = lax.rem(x_id + n_x - dx, n_x) * CORES + lax.rem(c_id + dc, CORES)
            block = pick(value, member)
            if dx or dc:
                perm = []
                for j in range(n_x):
                    for c in range(CORES):
                        source = ((j + dx) % n_x) * CORES + (c + dc) % CORES
                        perm.append((source, j * CORES + c))
                block = lax.ppermute(block, ("x", "c"), perm)
            out.append(block)
    return out


def shard_offsets():
    return [(dz, dy) for dz in range(Z) for dy in range(lax.axis_size("y"))]


def shard_permute(value, dz, dy, ahead):
    n_y = lax.axis_size("y")
    perm = []
    for z in range(Z):
        for y in range(n_y):
            far, near = ((z + dz) % Z) * n_y + (y + dy) % n_y, z * n_y + y
            perm.append((near, far) if ahead else (far, near))
    return lax.ppermute(value, ("z", "y"), perm)


def position_of(dz, dy):
    n_y = lax.axis_size("y")
    return lax.rem(lax.axis_index("z") + dz, Z) * n_y + lax.rem(lax.axis_index("y") + dy, n_y)


def ring_z(value):
    return [from_ahead(value, "z", k) if k else value for k in range(Z)]


def small_over_y(blocks):
    total = jnp.stack(blocks[0]).astype(F32)
    for k, group in enumerate(blocks[1:]):
        total = total + to_ahead(jnp.stack(group).astype(BF), "y", k + 1).astype(F32)
    return total


def small_over_z(total):
    low = total.astype(BF)
    return [total[0]] + [to_ahead(low[k], "z", k) for k in range(1, Z)]


def added(blocks):
    total = blocks[0]
    for block in blocks[1:]:
        total = total + block.astype(F32)
    return total


def after(values, done):
    return lax.optimization_barrier((values, done))[0]


def gather_z(value):
    return lax.all_gather(value, "z", axis=0, tiled=True)


def gather_shard(value):
    return lax.all_gather(value, ("z", "y"), axis=0, tiled=True)


def scatter_z(value):
    return lax.psum_scatter(value, "z", scatter_dimension=0, tiled=True)


def begin_reduce_y(value):
    n_y = lax.axis_size("y")
    index = lax.axis_index("y")
    blocks = value.astype(BF).reshape(Z, n_y, -1, value.shape[1])
    own = lax.dynamic_index_in_dim(blocks, index, axis=1, keepdims=False)
    others = []
    for k in range(1, n_y):
        block = lax.dynamic_index_in_dim(blocks, lax.rem(index + k, n_y), axis=1, keepdims=False)
        others.append(to_ahead(block, "y", k))
    return own, others


def end_reduce_y(own, others):
    total = own.astype(F32)
    for block in others:
        total = total + block.astype(F32)
    return total.astype(BF).reshape(-1, own.shape[-1])


def swap_y(wide):
    n_y = lax.axis_size("y")
    return [wide] + [from_ahead(wide, "y", k) for k in range(1, n_y)]


def merge_y(blocks, n):
    n_y = lax.axis_size("y")
    m = blocks[0].shape[1]
    blocks = [block.reshape(Z, 1, n, m) for block in blocks]
    if n_y == 2:
        first, second = blocks
        return jnp.where(
            lax.axis_index("y") == 0,
            jnp.concatenate([first, second], axis=1),
            jnp.concatenate([second, first], axis=1),
        ).reshape(-1, m)
    at = lax.rem(n_y - lax.axis_index("y"), n_y)
    stacked = jnp.concatenate(blocks + blocks[:-1], axis=1)
    return lax.dynamic_slice_in_dim(stacked, at, n_y, axis=1).reshape(-1, m)


def merge_own_y(blocks):
    n_y = lax.axis_size("y")
    if n_y == 2:
        first, second = blocks
        return jnp.where(
            lax.axis_index("y") == 0,
            jnp.concatenate([first, second]),
            jnp.concatenate([second, first]),
        )
    n = blocks[0].shape[0]
    at = lax.rem(n_y - lax.axis_index("y"), n_y) * n
    return lax.dynamic_slice_in_dim(jnp.concatenate(blocks + blocks[:-1]), at, n_y * n)


def reduce_own_y(value):
    n_y = lax.axis_size("y")
    index = lax.axis_index("y")
    blocks = value.reshape(n_y, -1, value.shape[1])
    total = lax.dynamic_index_in_dim(blocks, index, keepdims=False).astype(F32)
    for k in range(1, n_y):
        other = lax.dynamic_index_in_dim(blocks, lax.rem(index + k, n_y), keepdims=False)
        total = total + to_ahead(other, "y", k).astype(F32)
    return total.astype(BF)


def member_of(dc, dx):
    n_x = lax.axis_size("x")
    x_id = lax.rem(lax.axis_index("x") + dx, n_x)
    return x_id * CORES + lax.rem(lax.axis_index("c") + dc, CORES)


def offsets():
    return [(dc, dx) for dc in range(CORES) for dx in range(lax.axis_size("x"))]


def place_group(slots, axis, dtype):
    n = slots[0].shape[axis]
    shape = list(slots[0].shape)
    shape[axis] = n * len(slots)
    out = jnp.zeros(shape, dtype)
    for (dc, dx), slot in zip(offsets(), slots):
        start = [0] * len(shape)
        start[axis] = member_of(dc, dx) * n
        out = lax.dynamic_update_slice(out, slot.astype(dtype), start)
    return out


def spread_begin(wide):
    n_y, n_x = lax.axis_size("y"), lax.axis_size("x")
    over_y = [wide] + [from_ahead(wide, "y", k) for k in range(1, n_y)]
    over_x = [from_ahead(wide, "x", k) for k in range(1, n_x)]
    return over_y, over_x


def spread_next(over_y, over_x):
    n_x = lax.axis_size("x")
    return [[over_y[0]] + over_x] + [
        [block] + [from_ahead(block, "x", k) for k in range(1, n_x)] for block in over_y[1:]
    ]


def spread_end(grid):
    return [group + [from_ahead(block, "c", 1) for block in group] for group in grid]


def place_every(slots, n):
    n_y, n_x = lax.axis_size("y"), lax.axis_size("x")
    m = slots[0][0].shape[1]
    out = jnp.zeros((Z, n_y, n_x * CORES, n, m), BF)
    for ky, group in enumerate(slots):
        at_y = lax.rem(lax.axis_index("y") + ky, n_y)
        for (dc, dx), slot in zip(offsets(), group):
            out = lax.dynamic_update_slice(
                out, slot.reshape(Z, 1, 1, n, m), (0, at_y, member_of(dc, dx), 0, 0)
            )
    return out.reshape(-1, m)


def on_device(
    tokens,
    cotangent,
    lengths,
    attn_gain,
    query_down,
    key_value,
    query_gain,
    query_up,
    out_proj,
    mlp_gain,
    gate_up,
    down_proj,
):
    n_x = lax.axis_size("x")
    n_group = n_x * CORES
    n_y = lax.axis_size("y")
    n_shard = Z * n_y
    _, rows, width = tokens.shape
    rank = query_down.shape[1]
    group_id = lax.axis_index("x") * CORES + lax.axis_index("c")
    shard_id = lax.axis_index("z") * n_y + lax.axis_index("y")

    def quarter_rows(value):
        n = value.shape[0] // n_group
        return lax.dynamic_slice_in_dim(value, group_id * n, n, axis=0)

    def pick_cols(value, member):
        n = value.shape[1] // n_group
        return lax.dynamic_slice_in_dim(value, member * n, n, axis=1)

    def scaled(weight, gain):
        return (weight.astype(F32) * gain.astype(F32)[:, None]).astype(BF)

    def split(value):
        return [value[k * rows : (k + 1) * rows] for k in range(n_group)]

    qkv_own = jnp.concatenate([query_down, key_value], axis=1)
    qkv_ring = ring_z(scaled(pick_cols(qkv_own, group_id), attn_gain))
    qup_own = quarter_rows(scaled(query_up, query_gain))
    qup_mat = lax.all_gather(qup_own, ("z", "y", "x", "c"), axis=0, tiled=True)
    out_wide = gather_z(quarter_rows(out_proj))

    my_length = lax.dynamic_index_in_dim(lengths, group_id, keepdims=False)
    positions = shard_id * rows + jnp.arange(rows, dtype=jnp.int32)
    place = jnp.stack([lax.axis_index("z"), lax.axis_index("y")]).astype(jnp.int32)
    valid = (positions < my_length).astype(F32)[:, None]
    cosine, sine = rope_tables(positions, HD)

    x_rows = tokens[0].astype(F32)
    rms_first = inv_rms(x_rows)
    normed_first = x_rows * rms_first
    attn_input = normed_first.astype(BF)
    input_all = jnp.concatenate(gather_group(attn_input), axis=0)

    qkv_stack = jnp.stack(qkv_ring)
    qkv_grid = [qkv_stack] + [from_ahead(qkv_stack, "y", k) for k in range(1, n_y)]

    gate_up_late = after(gate_up, qkv_ring[1])
    gate_own, up_own = select_units(
        group_id.astype(jnp.int32).reshape(1),
        mlp_gain.astype(F32)[:, None],
        gate_up_late,
        n_shard,
        n_group,
    )
    gate_wide = gather_z(gate_own)

    qkv_mat = jnp.zeros((width, qkv_stack.shape[2]), BF)
    for dy, stack in enumerate(qkv_grid):
        for dz in range(Z):
            at = position_of(dz, dy) * stack.shape[1]
            qkv_mat = lax.dynamic_update_slice(qkv_mat, stack[dz], (at, 0))
    qkv_flat = matmul(input_all, qkv_mat)
    up_wide = gather_z(up_own)
    blocks = []
    for (dc, dx), block in zip(offsets(), split(qkv_flat)):
        if dc or dx:
            perm = []
            for j in range(n_x):
                for c in range(CORES):
                    target = ((j + dx) % n_x) * CORES + (c + dc) % CORES
                    perm.append((j * CORES + c, target))
            block = lax.ppermute(block, ("x", "c"), perm)
        blocks.append(block)
    qkv_out = jnp.zeros((rows, qkv_own.shape[1]), F32)
    n_cols = qkv_own.shape[1] // n_group
    for (dc, dx), block in zip(offsets(), blocks):
        member = lax.rem(lax.axis_index("x") + n_x - dx, n_x) * CORES
        member = member + lax.rem(lax.axis_index("c") + dc, CORES)
        qkv_out = lax.dynamic_update_slice(qkv_out, block, (0, member * n_cols))
    qdown_out, kv_out = qkv_out[:, :rank], qkv_out[:, rank:]

    key_rot = rotate(kv_out[:, :HD], cosine, sine).astype(BF)
    kv_local = jnp.concatenate([key_rot, kv_out[:, HD:].astype(BF)], axis=1)
    out_first = spread_begin(out_wide)
    kv_local = after(kv_local, out_wide)
    kv_ring = ring_z(kv_local)
    down_both = [quarter_rows(down_proj)]
    down_both += [from_ahead(after(down_both[0], qkv_flat), "y", k) for k in range(1, n_y)]
    down_mat = gather_z(merge_own_y(down_both))
    rms_query = inv_rms(qdown_out)
    normed_query = qdown_out * rms_query
    query_input = normed_query.astype(BF)
    kv_stack = jnp.stack(kv_ring)
    kv_grid = [kv_stack] + [from_ahead(kv_stack, "y", k) for k in range(1, n_y)]
    kv_grid = after(kv_grid, out_first)
    kv_whole = jnp.concatenate([stack[dz] for dz in range(Z) for stack in kv_grid])
    out_grid = spread_next(*out_first)
    query_rot, attn_low, logsum = attend(place, query_input, qup_mat, cosine, sine, kv_whole)
    gate_blocks = swap_y(gate_wide)
    out_slots = spread_end(after(out_grid, attn_low))
    out_mat = place_every(out_slots, out_proj.shape[0] // n_group)
    middle = x_rows + matmul(attn_low, out_mat)
    rms_second = inv_rms(middle)
    normed_second = middle * rms_second
    mlp_input = normed_second.astype(BF)

    mlp_all = jnp.concatenate(gather_group(mlp_input), axis=0)
    up_blocks = swap_y(up_wide)
    cot_rows = cotangent[0].astype(F32) * valid
    cot_late = after(cot_rows.astype(BF), mlp_input)
    cot_all = jnp.concatenate(gather_group(cot_late), axis=0)
    gate_mat = merge_y(after(gate_blocks, mlp_all), mlp_gain.shape[0])
    gate_part = matmul(mlp_all, gate_mat)
    up_mat = merge_y(after(up_blocks, (gate_part, down_mat)), mlp_gain.shape[0])
    def pick_out(value, member):
        parts = value.reshape(rows, n_shard, n_group, -1)
        return lax.dynamic_index_in_dim(parts, member, axis=2, keepdims=False).reshape(rows, -1)

    attn_late, query_late = after((attn_low, query_input), mlp_all)
    attn_all = jnp.concatenate(exchange_group(attn_late, pick_out), axis=0)
    query_all = jnp.concatenate(gather_group(query_late), axis=0)

    up_part = matmul(mlp_all, up_mat)
    sigmoid_gate = jax.nn.sigmoid(gate_part)
    activated = gate_part * sigmoid_gate
    hidden_low = (activated * up_part).astype(BF)

    down_term = contract_rows(hidden_low, cot_all).astype(BF)
    down_half = scatter_z(down_term)
    down_mat, down_term, attn_all, query_all = lax.optimization_barrier(
        (down_mat, down_term, attn_all, query_all)
    )
    hidden_grad = contract_cols(cot_all, down_mat)
    gate_grad = hidden_grad * up_part * (sigmoid_gate * (1.0 + gate_part * (1.0 - sigmoid_gate)))
    gate_low = gate_grad.astype(BF)
    up_low = (hidden_grad * activated).astype(BF)
    partial_in = contract_cols(gate_low, gate_mat) + contract_cols(up_low, up_mat)
    gate_low, up_low = after((gate_low, up_low), partial_in)
    gate_term = contract_rows(mlp_all, gate_low).astype(BF)
    gate_ends = begin_reduce_y(gate_term)
    up_term = contract_rows(mlp_all, after(up_low, gate_term)).astype(BF)
    up_half = scatter_z(up_term)
    mlp_in_grad = after(reduce_group(split(partial_in)), up_term)

    middle_grad = cot_rows + rms_second * (
        mlp_in_grad
        - normed_second * jnp.mean(mlp_in_grad * normed_second, axis=-1, keepdims=True)
    )
    middle_low = middle_grad.astype(BF)
    middle_all = jnp.concatenate(gather_group(middle_low), axis=0)
    attn_val_grad = contract_cols(middle_low, out_mat).astype(BF)
    query_raw_grad, kv_term = attend_back(
        place, query_rot, attn_val_grad, attn_low, logsum, cosine, sine, kv_whole
    )
    kv_slots = [kv_term[k * rows : (k + 1) * rows] for k in range(Z * n_y)]
    kv_near = small_over_y([kv_slots[k::n_y] for k in range(n_y)])
    kv_blocks = small_over_z(kv_near)
    gate_pre = end_reduce_y(gate_ends[0], after(gate_ends[1], kv_term))
    gate_sum = scatter_z(gate_pre)
    out_term = contract_rows(attn_all, after(middle_all, gate_pre)).astype(BF)
    out_ends = begin_reduce_y(out_term)
    kv_blocks, out_term = lax.optimization_barrier((kv_blocks, out_term))
    kv_grad = added(kv_blocks)
    raw_all = jnp.concatenate(exchange_group(query_raw_grad, pick_cols), axis=0)
    query_in_grad = contract_cols(query_raw_grad, qup_mat)
    qup_term = contract_rows(query_all, raw_all).astype(BF)
    qdown_grad = rms_query * (
        query_in_grad
        - normed_query * jnp.mean(query_in_grad * normed_query, axis=-1, keepdims=True)
    )
    kv_grad, qup_term = lax.optimization_barrier((kv_grad, qup_term))
    key_raw_grad = rotate_back(kv_grad[:, :HD], cosine, sine)
    qkv_low = jnp.concatenate([qdown_grad, key_raw_grad, kv_grad[:, HD:]], axis=1).astype(BF)
    qkv_parts, out_ends = lax.optimization_barrier(
        (exchange_group(qkv_low, pick_cols), out_ends)
    )
    out_pre = end_reduce_y(*out_ends)
    out_sum = scatter_z(out_pre)
    qkv_all = jnp.concatenate(after(qkv_parts, out_pre), axis=0)
    qkv_term = contract_rows(input_all, qkv_all).astype(BF)
    n_own = query_down.shape[0]
    qkv_near = small_over_y(
        [
            [
                lax.dynamic_slice_in_dim(qkv_term, position_of(dz, dy) * n_own, n_own)
                for dz in range(Z)
            ]
            for dy in range(n_y)
        ]
    )
    first_part = contract_cols(after(qkv_all, qkv_term), qkv_mat)
    first_in_grad = reduce_group(split(first_part))
    qup_ends = begin_reduce_y(after(qup_term, out_ends))
    layer_part = matmul(after(hidden_low, first_part), down_mat)
    down_sum = reduce_own_y(after(down_half, layer_part))
    up_sum = reduce_own_y(after(up_half, down_half))
    qup_ends, first_in_grad, layer_part, up_sum = lax.optimization_barrier(
        (qup_ends, first_in_grad, layer_part, up_sum)
    )
    qup_pre = end_reduce_y(*qup_ends)
    qup_sum = scatter_z(qup_pre)
    layer_sum = reduce_group(split(layer_part))
    up_slots = gather_group(up_sum)
    gate_slots = gather_group(after(gate_sum, up_sum))
    down_slots = gather_group(down_sum)
    qkv_blocks = small_over_z(qkv_near)
    qkv_blocks, up_slots, gate_slots = lax.optimization_barrier(
        (qkv_blocks, up_slots, gate_slots)
    )
    input_rows_grad = middle_grad + rms_first * (
        first_in_grad
        - normed_first * jnp.mean(first_in_grad * normed_first, axis=-1, keepdims=True)
    )
    order = jnp.zeros((n_group,), jnp.int32)
    for k, (dc, dx) in enumerate(offsets()):
        order = order.at[member_of(dc, dx)].set(k)
    gateup_grad, second_gain_grad = interleave(
        order, mlp_gain.astype(F32)[:, None], gate_up, gate_slots, up_slots, n_shard
    )
    qkv_blocks, gateup_grad, layer_sum, down_slots = lax.optimization_barrier(
        (qkv_blocks, gateup_grad, layer_sum, down_slots)
    )
    qkv_sum = added(qkv_blocks).astype(BF)
    layer = (middle + layer_sum) * valid
    out_slots = gather_group(after(out_sum, gate_slots))

    down_grad = place_group(down_slots, 0, F32)
    out_grad = place_group(out_slots, 0, F32)
    qup_raw = place_group(gather_group(after(qup_sum, out_slots)), 1, F32)
    qkv_raw = place_group(gather_group(qkv_sum), 1, F32)

    def gain_grad(weight, grad):
        return jnp.sum(weight.astype(F32) * grad, axis=1)

    qkv_weight_grad = qkv_raw * attn_gain.astype(F32)[:, None]
    return (
        layer.astype(BF)[None],
        input_rows_grad.astype(BF)[None],
        gain_grad(qkv_own, qkv_raw),
        qkv_weight_grad[:, :rank],
        qkv_weight_grad[:, rank:],
        gain_grad(query_up, qup_raw),
        qup_raw * query_gain.astype(F32)[:, None],
        out_grad,
        second_gain_grad[:, 0],
        gateup_grad,
        down_grad,
    )


def solution(mesh):
    n_replica, n_shard = mesh.devices.shape
    devices = mesh.devices.reshape(n_replica // CORES, CORES, Z, n_shard // Z)
    inner = Mesh(devices, ("x", "c", "z", "y"))
    group, shard = ("x", "c"), ("z", "y")
    acts = P(group, shard, None)
    vec = P(shard)
    mat = P(shard, None)
    in_specs = (acts, acts, P(), vec, mat, mat, vec, mat, mat, vec, mat, mat)
    out_specs = (acts, acts, vec, mat, mat, vec, mat, mat, vec, mat, mat)
    return jax.shard_map(
        on_device, mesh=inner, in_specs=in_specs, out_specs=out_specs, check_vma=False
    )
```

```python
import math

import jax
import jax.numpy as jnp
from jax import lax
from jax.experimental import pallas as pl
from jax.experimental.pallas import tpu as pltpu
from jax.sharding import Mesh
from jax.sharding import PartitionSpec as P

HEADS = 16
HD = 256
FF = 5632
Z = 4
CORES = 2


EPSILON = 1e-06
BF = jnp.bfloat16
F32 = jnp.float32


def inv_rms(values):
    return lax.rsqrt(jnp.mean(values * values, axis=-1, keepdims=True) + EPSILON)


def rope_tables(positions, head_dim):
    half_dim = head_dim // 2
    frequency = jnp.exp(-math.log(10000.0) * jnp.arange(half_dim).astype(F32) / half_dim)
    angles = positions.astype(F32)[:, None] * frequency[None, :]
    return (jnp.cos(angles), jnp.sin(angles))


def rotate(values, cosine, sine):
    half_dim = values.shape[-1] // 2
    first_half = values[..., :half_dim]
    second_half = values[..., half_dim:]
    return jnp.concatenate(
        [first_half * cosine - second_half * sine, second_half * cosine + first_half * sine],
        axis=-1,
    )


def rotate_back(grads, cosine, sine):
    half_dim = grads.shape[-1] // 2
    first_half = grads[..., :half_dim]
    second_half = grads[..., half_dim:]
    return jnp.concatenate(
        [first_half * cosine + second_half * sine, second_half * cosine - first_half * sine],
        axis=-1,
    )


def matmul(left, right):
    return jnp.dot(left, right, preferred_element_type=F32)


def contract_rows(left, right):
    return lax.dot_general(left, right, (((0,), (0,)), ((), ())), preferred_element_type=F32)


def contract_cols(left, right):
    return lax.dot_general(left, right, (((1,), (1,)), ((), ())), preferred_element_type=F32)


STEP_HEADS = 4
LIGHT = 1000
NEG = -1e30


def dot_last(left, right):
    return lax.dot_general(left, right, (((1,), (1,)), ((), ())), preferred_element_type=F32)


def seen(shape, rows, y_index):
    n_y = shape[0] // rows
    key = lax.broadcasted_iota(jnp.int32, shape, 0)
    row = lax.broadcasted_iota(jnp.int32, shape, 1)
    ahead = key // rows
    block = lax.rem(y_index + ahead, n_y)
    return (block - y_index) * rows + key - ahead * rows <= row


def attend_kernel(
    place_ref, input_ref, up_ref, cos_ref, sin_ref, kv_ref, q_ref, o_ref, lse_ref,
    vt_ref, m_ref, l_ref, acc_ref,
):
    rows = input_ref.shape[0]
    chunk_rows = kv_ref.shape[0] // Z
    half = HD // 2

    @pl.when(pl.program_id(0) == 0)
    def _():
        for c in range(Z):
            at = slice(c * chunk_rows, (c + 1) * chunk_rows)
            vt_ref[:, at] = kv_ref[at, HD:].T

    cosine, sine = cos_ref[...], sin_ref[...]
    scale = 1.0 / math.sqrt(HD)
    raw = matmul(input_ref[...], up_ref[...])
    for j in range(STEP_HEADS):
        first, second = raw[:, j * HD : j * HD + half], raw[:, j * HD + half : (j + 1) * HD]
        turned = jnp.concatenate(
            [first * cosine - second * sine, second * cosine + first * sine], axis=1
        )
        q_ref[:, j * HD : (j + 1) * HD] = (turned.astype(BF).astype(F32) * scale).astype(BF)
    m_ref[...] = jnp.full_like(m_ref, NEG)
    l_ref[...] = jnp.zeros_like(l_ref)
    acc_ref[...] = jnp.zeros_like(acc_ref)

    def chunk(c, masked):
        at = pl.multiple_of(c * chunk_rows, chunk_rows)
        keys = kv_ref[pl.ds(at, chunk_rows), :HD]
        values = vt_ref[:, pl.ds(at, chunk_rows)]
        for j in range(STEP_HEADS):
            scores = dot_last(keys, q_ref[:, j * HD : (j + 1) * HD])
            if masked:
                scores = jnp.where(seen(scores.shape, rows, place_ref[1]), scores, NEG)
            peak = jnp.maximum(m_ref[j], jnp.max(scores, axis=0, keepdims=True))
            alpha = jnp.exp(m_ref[j] - peak)
            expo = jnp.exp(scores - peak)
            m_ref[j] = peak
            l_ref[j] = l_ref[j] * alpha + jnp.sum(expo, axis=0, keepdims=True)
            acc_ref[j] = acc_ref[j] * alpha + matmul(values, expo.astype(BF))

    @pl.loop(Z - place_ref[0], Z)
    def _(c):
        chunk(c, False)

    chunk(0, True)
    for j in range(STEP_HEADS):
        o_ref[:, j * HD : (j + 1) * HD] = (acc_ref[j] / l_ref[j]).T.astype(BF)
        lse_ref[j] = m_ref[j] + jnp.log(l_ref[j])


def attend(place, query_input, up_mat, cosine, sine, kv_whole):
    rows, rank = query_input.shape
    slot_len = kv_whole.shape[0]
    wide = STEP_HEADS * HD
    whole = lambda h, *_: (0, 0)
    by_head = lambda h, *_: (0, h)
    return pl.pallas_call(
        attend_kernel,
        out_shape=(
            jax.ShapeDtypeStruct((rows, HEADS * HD), BF),
            jax.ShapeDtypeStruct((rows, HEADS * HD), BF),
            jax.ShapeDtypeStruct((HEADS, 1, rows), F32),
        ),
        grid_spec=pltpu.PrefetchScalarGridSpec(
            num_scalar_prefetch=1,
            grid=(HEADS // STEP_HEADS,),
            in_specs=[
                pl.BlockSpec((rows, rank), whole),
                pl.BlockSpec((rank, wide), by_head),
                pl.BlockSpec((rows, HD // 2), whole),
                pl.BlockSpec((rows, HD // 2), whole),
                pl.BlockSpec((slot_len, 2 * HD), whole),
            ],
            out_specs=[
                pl.BlockSpec((rows, wide), by_head),
                pl.BlockSpec((rows, wide), by_head),
                pl.BlockSpec((STEP_HEADS, 1, rows), lambda h, *_: (h, 0, 0)),
            ],
            scratch_shapes=[
                pltpu.VMEM((HD, slot_len), BF),
                pltpu.VMEM((STEP_HEADS, 1, rows), F32),
                pltpu.VMEM((STEP_HEADS, 1, rows), F32),
                pltpu.VMEM((STEP_HEADS, HD, rows), F32),
            ],
        ),
        compiler_params=pltpu.CompilerParams(
            dimension_semantics=("arbitrary",), vmem_limit_bytes=40 * 1024 * 1024
        ),
        cost_estimate=pl.CostEstimate(
            flops=LIGHT, bytes_accessed=LIGHT, transcendentals=0
        ),
    )(place, query_input, up_mat, cosine, sine, kv_whole)


def attend_back_kernel(
    place_ref, q_ref, do_ref, o_ref, lse_ref, cos_ref, sin_ref, kv_ref, dq_ref, dkv_ref,
    acc_ref, dqs_ref,
):
    rows = q_ref.shape[0]
    chunk_rows = kv_ref.shape[0] // Z
    half = HD // 2
    step = pl.program_id(0)

    @pl.when(step == 0)
    def _():
        acc_ref[...] = jnp.zeros_like(acc_ref)

    dqs_ref[...] = jnp.zeros_like(dqs_ref)
    deltas = []
    for j in range(STEP_HEADS):
        at = slice(j * HD, (j + 1) * HD)
        prod = do_ref[:, at].astype(F32) * o_ref[:, at].astype(F32)
        deltas.append(jnp.sum(prod.T, axis=0, keepdims=True))

    def chunk(c, masked):
        at = pl.ds(pl.multiple_of(c * chunk_rows, chunk_rows), chunk_rows)
        keys = kv_ref[at, :HD]
        values = kv_ref[at, HD:]
        for j in range(STEP_HEADS):
            query = q_ref[:, j * HD : (j + 1) * HD]
            out_grad = do_ref[:, j * HD : (j + 1) * HD]
            probs = jnp.exp(dot_last(keys, query) - lse_ref[j])
            if masked:
                probs = jnp.where(seen(probs.shape, rows, place_ref[1]), probs, 0.0)
            score_grad = (probs * (dot_last(values, out_grad) - deltas[j])).astype(BF)
            acc_ref[at, HD:] += matmul(probs.astype(BF), out_grad)
            acc_ref[at, :HD] += matmul(score_grad, query)
            dqs_ref[j] += contract_rows(score_grad, keys)

    @pl.loop(Z - place_ref[0], Z)
    def _(c):
        chunk(c, False)

    chunk(0, True)
    cosine, sine = cos_ref[...], sin_ref[...]
    scale = 1.0 / math.sqrt(HD)
    for j in range(STEP_HEADS):
        first, second = dqs_ref[j, :, :half] * scale, dqs_ref[j, :, half:] * scale
        dq_ref[:, j * HD : (j + 1) * HD] = jnp.concatenate(
            [first * cosine + second * sine, second * cosine - first * sine], axis=1
        ).astype(BF)

    @pl.when(step == pl.num_programs(0) - 1)
    def _():
        dkv_ref[...] = acc_ref[...].astype(BF)


def attend_back(place, query, out_grad, attn_low, logsum, cosine, sine, kv_whole):
    rows = query.shape[0]
    slot_len = kv_whole.shape[0]
    wide = STEP_HEADS * HD
    whole = lambda h, *_: (0, 0)
    by_head = lambda h, *_: (0, h)
    return pl.pallas_call(
        attend_back_kernel,
        out_shape=(
            jax.ShapeDtypeStruct((rows, HEADS * HD), BF),
            jax.ShapeDtypeStruct((slot_len, 2 * HD), BF),
        ),
        grid_spec=pltpu.PrefetchScalarGridSpec(
            num_scalar_prefetch=1,
            grid=(HEADS // STEP_HEADS,),
            in_specs=[
                pl.BlockSpec((rows, wide), by_head),
                pl.BlockSpec((rows, wide), by_head),
                pl.BlockSpec((rows, wide), by_head),
                pl.BlockSpec((STEP_HEADS, 1, rows), lambda h, *_: (h, 0, 0)),
                pl.BlockSpec((rows, HD // 2), whole),
                pl.BlockSpec((rows, HD // 2), whole),
                pl.BlockSpec((slot_len, 2 * HD), whole),
            ],
            out_specs=[
                pl.BlockSpec((rows, wide), by_head),
                pl.BlockSpec((slot_len, 2 * HD), whole),
            ],
            scratch_shapes=[
                pltpu.VMEM((slot_len, 2 * HD), F32),
                pltpu.VMEM((STEP_HEADS, rows, HD), F32),
            ],
        ),
        compiler_params=pltpu.CompilerParams(
            dimension_semantics=("arbitrary",), vmem_limit_bytes=40 * 1024 * 1024
        ),
        cost_estimate=pl.CostEstimate(
            flops=LIGHT, bytes_accessed=LIGHT, transcendentals=0
        ),
    )(place, query, out_grad, attn_low, logsum, cosine, sine, kv_whole)


def interleave_kernel(n_shard, order_ref, gain_ref, weight_ref, *refs):
    *slot_refs, out_ref, sum_ref = refs
    n_group = len(slot_refs) // 2
    part = slot_refs[0].shape[1]
    unit = part // n_shard
    width = part * n_group
    total = 0.0
    gain = gain_ref[...]
    for half in range(2):
        slots = [ref[...].astype(F32) for ref in slot_refs[half * n_group : (half + 1) * n_group]]
        blocks = []
        for member in range(n_group):
            block = slots[0]
            for k in range(1, n_group):
                block = jnp.where(order_ref[member] == k, slots[k], block)
            blocks.append(block)
        row = jnp.concatenate(
            [
                blocks[member][:, s * unit : (s + 1) * unit]
                for s in range(n_shard)
                for member in range(n_group)
            ],
            axis=1,
        )
        at = slice(half * width, (half + 1) * width)
        total = total + jnp.sum(row * weight_ref[:, at].astype(F32), axis=1, keepdims=True)
        out_ref[:, at] = row * gain
    sum_ref[...] = total


def interleave(order, gain, weight, gate_slots, up_slots, n_shard):
    rows, width = weight.shape
    block = 32
    slots = [*gate_slots, *up_slots]
    by_row = lambda i, *_: (i, 0)
    return pl.pallas_call(
        lambda *refs: interleave_kernel(n_shard, *refs),
        out_shape=(
            jax.ShapeDtypeStruct((rows, width), F32),
            jax.ShapeDtypeStruct((rows, 1), F32),
        ),
        grid_spec=pltpu.PrefetchScalarGridSpec(
            num_scalar_prefetch=1,
            grid=(rows // block,),
            in_specs=[
                pl.BlockSpec((block, 1), by_row),
                pl.BlockSpec((block, width), by_row),
                *[pl.BlockSpec((block, slots[0].shape[1]), by_row) for _ in slots],
            ],
            out_specs=[
                pl.BlockSpec((block, width), by_row),
                pl.BlockSpec((block, 1), by_row),
            ],
        ),
        compiler_params=pltpu.CompilerParams(dimension_semantics=("arbitrary",)),
        cost_estimate=pl.CostEstimate(flops=LIGHT, bytes_accessed=LIGHT, transcendentals=0),
    )(order, gain, weight, *slots)


def select_kernel(n_shard, n_group, member_ref, gain_ref, weight_ref, gate_ref, up_ref):
    width = weight_ref.shape[1] // 2
    unit = width // n_shard // n_group
    gain = gain_ref[...]
    for half, out_ref in enumerate((gate_ref, up_ref)):
        pieces = []
        for s in range(n_shard):
            at = half * width + s * n_group * unit
            piece = weight_ref[:, at : at + unit].astype(F32)
            for k in range(1, n_group):
                other = weight_ref[:, at + k * unit : at + (k + 1) * unit].astype(F32)
                piece = jnp.where(member_ref[0] == k, other, piece)
            pieces.append(piece)
        out_ref[...] = (jnp.concatenate(pieces, axis=1) * gain).astype(BF)


def select_units(member, gain, weight, n_shard, n_group):
    rows, width = weight.shape
    block = 32
    part = width // 2 // n_group
    by_row = lambda i, *_: (i, 0)
    return pl.pallas_call(
        lambda *refs: select_kernel(n_shard, n_group, *refs),
        out_shape=(jax.ShapeDtypeStruct((rows, part), BF),) * 2,
        grid_spec=pltpu.PrefetchScalarGridSpec(
            num_scalar_prefetch=1,
            grid=(rows // block,),
            in_specs=[
                pl.BlockSpec((block, 1), by_row),
                pl.BlockSpec((block, width), by_row),
            ],
            out_specs=[pl.BlockSpec((block, part), by_row)] * 2,
        ),
        compiler_params=pltpu.CompilerParams(dimension_semantics=("arbitrary",)),
        cost_estimate=pl.CostEstimate(flops=LIGHT, bytes_accessed=LIGHT, transcendentals=0),
    )(member, gain, weight)


def from_ahead(value, axis, step):
    n = lax.axis_size(axis)
    return lax.ppermute(value, axis, [((j + step) % n, j) for j in range(n)])


def to_ahead(value, axis, step):
    n = lax.axis_size(axis)
    return lax.ppermute(value, axis, [(j, (j + step) % n) for j in range(n)])


def gather_group(value):
    n_x = lax.axis_size("x")
    mine = [value] + [from_ahead(value, "x", k) for k in range(1, n_x)]
    return mine + [from_ahead(v, "c", 1) for v in mine]


def reduce_group(parts):
    n_x = lax.axis_size("x")
    near, far = parts[:n_x], parts[n_x:]
    sums = [a + to_ahead(b.astype(BF), "c", 1).astype(F32) for a, b in zip(near, far)]
    total = sums[0]
    for k in range(1, n_x):
        total = total + to_ahead(sums[k].astype(BF), "x", k).astype(F32)
    return total


def exchange_group(value, pick):
    n_x = lax.axis_size("x")
    x_id, c_id = lax.axis_index("x"), lax.axis_index("c")
    out = []
    for dc in range(CORES):
        for dx in range(n_x):
            member = lax.rem(x_id + n_x - dx, n_x) * CORES + lax.rem(c_id + dc, CORES)
            block = pick(value, member)
            if dx or dc:
                perm = []
                for j in range(n_x):
                    for c in range(CORES):
                        source = ((j + dx) % n_x) * CORES + (c + dc) % CORES
                        perm.append((source, j * CORES + c))
                block = lax.ppermute(block, ("x", "c"), perm)
            out.append(block)
    return out


def shard_offsets():
    return [(dz, dy) for dz in range(Z) for dy in range(lax.axis_size("y"))]


def shard_permute(value, dz, dy, ahead):
    n_y = lax.axis_size("y")
    perm = []
    for z in range(Z):
        for y in range(n_y):
            far, near = ((z + dz) % Z) * n_y + (y + dy) % n_y, z * n_y + y
            perm.append((near, far) if ahead else (far, near))
    return lax.ppermute(value, ("z", "y"), perm)


def position_of(dz, dy):
    n_y = lax.axis_size("y")
    return lax.rem(lax.axis_index("z") + dz, Z) * n_y + lax.rem(lax.axis_index("y") + dy, n_y)


def ring_z(value):
    return [from_ahead(value, "z", k) if k else value for k in range(Z)]


def small_over_y(blocks):
    total = jnp.stack(blocks[0]).astype(F32)
    for k, group in enumerate(blocks[1:]):
        total = total + to_ahead(jnp.stack(group).astype(BF), "y", k + 1).astype(F32)
    return total


def small_over_z(total):
    low = total.astype(BF)
    return [total[0]] + [to_ahead(low[k], "z", k) for k in range(1, Z)]


def added(blocks):
    total = blocks[0]
    for block in blocks[1:]:
        total = total + block.astype(F32)
    return total


def after(values, done):
    return lax.optimization_barrier((values, done))[0]


def gather_z(value):
    return lax.all_gather(value, "z", axis=0, tiled=True)


def gather_shard(value):
    return lax.all_gather(value, ("z", "y"), axis=0, tiled=True)


def scatter_z(value):
    return lax.psum_scatter(value, "z", scatter_dimension=0, tiled=True)


def begin_reduce_y(value):
    n_y = lax.axis_size("y")
    index = lax.axis_index("y")
    blocks = value.astype(BF).reshape(Z, n_y, -1, value.shape[1])
    own = lax.dynamic_index_in_dim(blocks, index, axis=1, keepdims=False)
    others = []
    for k in range(1, n_y):
        block = lax.dynamic_index_in_dim(blocks, lax.rem(index + k, n_y), axis=1, keepdims=False)
        others.append(to_ahead(block, "y", k))
    return own, others


def end_reduce_y(own, others):
    total = own.astype(F32)
    for block in others:
        total = total + block.astype(F32)
    return total.astype(BF).reshape(-1, own.shape[-1])


def swap_y(wide):
    n_y = lax.axis_size("y")
    return [wide] + [from_ahead(wide, "y", k) for k in range(1, n_y)]


def merge_y(blocks, n):
    n_y = lax.axis_size("y")
    m = blocks[0].shape[1]
    blocks = [block.reshape(Z, 1, n, m) for block in blocks]
    if n_y == 2:
        first, second = blocks
        return jnp.where(
            lax.axis_index("y") == 0,
            jnp.concatenate([first, second], axis=1),
            jnp.concatenate([second, first], axis=1),
        ).reshape(-1, m)
    at = lax.rem(n_y - lax.axis_index("y"), n_y)
    stacked = jnp.concatenate(blocks + blocks[:-1], axis=1)
    return lax.dynamic_slice_in_dim(stacked, at, n_y, axis=1).reshape(-1, m)


def merge_own_y(blocks):
    n_y = lax.axis_size("y")
    if n_y == 2:
        first, second = blocks
        return jnp.where(
            lax.axis_index("y") == 0,
            jnp.concatenate([first, second]),
            jnp.concatenate([second, first]),
        )
    n = blocks[0].shape[0]
    at = lax.rem(n_y - lax.axis_index("y"), n_y) * n
    return lax.dynamic_slice_in_dim(jnp.concatenate(blocks + blocks[:-1]), at, n_y * n)


def reduce_own_y(value):
    n_y = lax.axis_size("y")
    index = lax.axis_index("y")
    blocks = value.reshape(n_y, -1, value.shape[1])
    total = lax.dynamic_index_in_dim(blocks, index, keepdims=False).astype(F32)
    for k in range(1, n_y):
        other = lax.dynamic_index_in_dim(blocks, lax.rem(index + k, n_y), keepdims=False)
        total = total + to_ahead(other, "y", k).astype(F32)
    return total.astype(BF)


def member_of(dc, dx):
    n_x = lax.axis_size("x")
    x_id = lax.rem(lax.axis_index("x") + dx, n_x)
    return x_id * CORES + lax.rem(lax.axis_index("c") + dc, CORES)


def offsets():
    return [(dc, dx) for dc in range(CORES) for dx in range(lax.axis_size("x"))]


def place_group(slots, axis, dtype):
    n = slots[0].shape[axis]
    shape = list(slots[0].shape)
    shape[axis] = n * len(slots)
    out = jnp.zeros(shape, dtype)
    for (dc, dx), slot in zip(offsets(), slots):
        start = [0] * len(shape)
        start[axis] = member_of(dc, dx) * n
        out = lax.dynamic_update_slice(out, slot.astype(dtype), start)
    return out


def spread_begin(wide):
    n_y, n_x = lax.axis_size("y"), lax.axis_size("x")
    over_y = [wide] + [from_ahead(wide, "y", k) for k in range(1, n_y)]
    over_x = [from_ahead(wide, "x", k) for k in range(1, n_x)]
    return over_y, over_x


def spread_next(over_y, over_x):
    n_x = lax.axis_size("x")
    return [[over_y[0]] + over_x] + [
        [block] + [from_ahead(block, "x", k) for k in range(1, n_x)] for block in over_y[1:]
    ]


def spread_end(grid):
    return [group + [from_ahead(block, "c", 1) for block in group] for group in grid]


def place_every(slots, n):
    n_y, n_x = lax.axis_size("y"), lax.axis_size("x")
    m = slots[0][0].shape[1]
    out = jnp.zeros((Z, n_y, n_x * CORES, n, m), BF)
    for ky, group in enumerate(slots):
        at_y = lax.rem(lax.axis_index("y") + ky, n_y)
        for (dc, dx), slot in zip(offsets(), group):
            out = lax.dynamic_update_slice(
                out, slot.reshape(Z, 1, 1, n, m), (0, at_y, member_of(dc, dx), 0, 0)
            )
    return out.reshape(-1, m)


def on_device(
    tokens,
    cotangent,
    lengths,
    attn_gain,
    query_down,
    key_value,
    query_gain,
    query_up,
    out_proj,
    mlp_gain,
    gate_up,
    down_proj,
):
    n_x = lax.axis_size("x")
    n_group = n_x * CORES
    n_y = lax.axis_size("y")
    n_shard = Z * n_y
    _, rows, width = tokens.shape
    rank = query_down.shape[1]
    group_id = lax.axis_index("x") * CORES + lax.axis_index("c")
    shard_id = lax.axis_index("z") * n_y + lax.axis_index("y")

    def quarter_rows(value):
        n = value.shape[0] // n_group
        return lax.dynamic_slice_in_dim(value, group_id * n, n, axis=0)

    def pick_cols(value, member):
        n = value.shape[1] // n_group
        return lax.dynamic_slice_in_dim(value, member * n, n, axis=1)

    def scaled(weight, gain):
        return (weight.astype(F32) * gain.astype(F32)[:, None]).astype(BF)

    def split(value):
        return [value[k * rows : (k + 1) * rows] for k in range(n_group)]

    qkv_own = jnp.concatenate([query_down, key_value], axis=1)
    qkv_ring = ring_z(scaled(pick_cols(qkv_own, group_id), attn_gain))
    qup_own = quarter_rows(scaled(query_up, query_gain))
    qup_mat = lax.all_gather(qup_own, ("z", "y", "x", "c"), axis=0, tiled=True)
    out_wide = gather_z(quarter_rows(out_proj))

    my_length = lax.dynamic_index_in_dim(lengths, group_id, keepdims=False)
    positions = shard_id * rows + jnp.arange(rows, dtype=jnp.int32)
    place = jnp.stack([lax.axis_index("z"), lax.axis_index("y")]).astype(jnp.int32)
    valid = (positions < my_length).astype(F32)[:, None]
    cosine, sine = rope_tables(positions, HD)

    x_rows = tokens[0].astype(F32)
    rms_first = inv_rms(x_rows)
    normed_first = x_rows * rms_first
    attn_input = normed_first.astype(BF)
    input_all = jnp.concatenate(gather_group(attn_input), axis=0)

    qkv_stack = jnp.stack(qkv_ring)
    qkv_grid = [qkv_stack] + [from_ahead(qkv_stack, "y", k) for k in range(1, n_y)]

    gate_up_late = after(gate_up, qkv_ring[1])
    gate_own, up_own = select_units(
        group_id.astype(jnp.int32).reshape(1),
        mlp_gain.astype(F32)[:, None],
        gate_up_late,
        n_shard,
        n_group,
    )
    gate_wide = gather_z(gate_own)

    qkv_mat = jnp.zeros((width, qkv_stack.shape[2]), BF)
    for dy, stack in enumerate(qkv_grid):
        for dz in range(Z):
            at = position_of(dz, dy) * stack.shape[1]
            qkv_mat = lax.dynamic_update_slice(qkv_mat, stack[dz], (at, 0))
    qkv_flat = matmul(input_all, qkv_mat)
    up_wide = gather_z(up_own)
    blocks = []
    for (dc, dx), block in zip(offsets(), split(qkv_flat)):
        if dc or dx:
            perm = []
            for j in range(n_x):
                for c in range(CORES):
                    target = ((j + dx) % n_x) * CORES + (c + dc) % CORES
                    perm.append((j * CORES + c, target))
            block = lax.ppermute(block, ("x", "c"), perm)
        blocks.append(block)
    qkv_out = jnp.zeros((rows, qkv_own.shape[1]), F32)
    n_cols = qkv_own.shape[1] // n_group
    for (dc, dx), block in zip(offsets(), blocks):
        member = lax.rem(lax.axis_index("x") + n_x - dx, n_x) * CORES
        member = member + lax.rem(lax.axis_index("c") + dc, CORES)
        qkv_out = lax.dynamic_update_slice(qkv_out, block, (0, member * n_cols))
    qdown_out, kv_out = qkv_out[:, :rank], qkv_out[:, rank:]

    key_rot = rotate(kv_out[:, :HD], cosine, sine).astype(BF)
    kv_local = jnp.concatenate([key_rot, kv_out[:, HD:].astype(BF)], axis=1)
    out_first = spread_begin(out_wide)
    kv_local = after(kv_local, out_wide)
    kv_ring = ring_z(kv_local)
    down_both = [quarter_rows(down_proj)]
    down_both += [from_ahead(after(down_both[0], qkv_flat), "y", k) for k in range(1, n_y)]
    down_mat = gather_z(merge_own_y(down_both))
    rms_query = inv_rms(qdown_out)
    normed_query = qdown_out * rms_query
    query_input = normed_query.astype(BF)
    kv_stack = jnp.stack(kv_ring)
    kv_grid = [kv_stack] + [from_ahead(kv_stack, "y", k) for k in range(1, n_y)]
    kv_grid = after(kv_grid, out_first)
    kv_whole = jnp.concatenate([stack[dz] for dz in range(Z) for stack in kv_grid])
    out_grid = spread_next(*out_first)
    query_rot, attn_low, logsum = attend(place, query_input, qup_mat, cosine, sine, kv_whole)
    gate_blocks = swap_y(gate_wide)
    out_slots = spread_end(after(out_grid, attn_low))
    out_mat = place_every(out_slots, out_proj.shape[0] // n_group)
    middle = x_rows + matmul(attn_low, out_mat)
    rms_second = inv_rms(middle)
    normed_second = middle * rms_second
    mlp_input = normed_second.astype(BF)

    mlp_all = jnp.concatenate(gather_group(mlp_input), axis=0)
    up_blocks = swap_y(up_wide)
    cot_rows = cotangent[0].astype(F32) * valid
    cot_late = after(cot_rows.astype(BF), mlp_input)
    cot_all = jnp.concatenate(gather_group(cot_late), axis=0)
    gate_mat = merge_y(after(gate_blocks, mlp_all), mlp_gain.shape[0])
    gate_part = matmul(mlp_all, gate_mat)
    up_mat = merge_y(after(up_blocks, (gate_part, down_mat)), mlp_gain.shape[0])
    def pick_out(value, member):
        parts = value.reshape(rows, n_shard, n_group, -1)
        return lax.dynamic_index_in_dim(parts, member, axis=2, keepdims=False).reshape(rows, -1)

    attn_late, query_late = after((attn_low, query_input), mlp_all)
    attn_all = jnp.concatenate(exchange_group(attn_late, pick_out), axis=0)
    query_all = jnp.concatenate(gather_group(query_late), axis=0)

    up_mat, attn_all, query_all = lax.optimization_barrier((up_mat, attn_all, query_all))
    up_part = matmul(mlp_all, up_mat)
    sigmoid_gate = jax.nn.sigmoid(gate_part)
    activated = gate_part * sigmoid_gate
    hidden_low = (activated * up_part).astype(BF)

    down_term = contract_rows(hidden_low, cot_all).astype(BF)
    down_half = scatter_z(down_term)
    down_mat = after(down_mat, down_term)
    hidden_grad = contract_cols(cot_all, down_mat)
    gate_grad = hidden_grad * up_part * (sigmoid_gate * (1.0 + gate_part * (1.0 - sigmoid_gate)))
    gate_low = gate_grad.astype(BF)
    up_low = (hidden_grad * activated).astype(BF)
    partial_in = contract_cols(gate_low, gate_mat) + contract_cols(up_low, up_mat)
    gate_low, up_low = after((gate_low, up_low), partial_in)
    gate_term = contract_rows(mlp_all, gate_low).astype(BF)
    gate_ends = begin_reduce_y(gate_term)
    up_term = contract_rows(mlp_all, after(up_low, gate_term)).astype(BF)
    up_half = scatter_z(up_term)
    mlp_in_grad = after(reduce_group(split(partial_in)), up_term)

    middle_grad = cot_rows + rms_second * (
        mlp_in_grad
        - normed_second * jnp.mean(mlp_in_grad * normed_second, axis=-1, keepdims=True)
    )
    middle_low = middle_grad.astype(BF)
    middle_all = jnp.concatenate(gather_group(middle_low), axis=0)
    attn_val_grad = contract_cols(middle_low, out_mat).astype(BF)
    query_raw_grad, kv_term = attend_back(
        place, query_rot, attn_val_grad, attn_low, logsum, cosine, sine, kv_whole
    )
    kv_slots = [kv_term[k * rows : (k + 1) * rows] for k in range(Z * n_y)]
    kv_near = small_over_y([kv_slots[k::n_y] for k in range(n_y)])
    kv_blocks = small_over_z(kv_near)
    gate_pre = end_reduce_y(gate_ends[0], after(gate_ends[1], kv_term))
    gate_sum = scatter_z(gate_pre)
    out_term = contract_rows(attn_all, after(middle_all, gate_pre)).astype(BF)
    out_ends = begin_reduce_y(out_term)
    kv_blocks, out_term = lax.optimization_barrier((kv_blocks, out_term))
    kv_grad = added(kv_blocks)
    raw_all = jnp.concatenate(exchange_group(query_raw_grad, pick_cols), axis=0)
    query_in_grad = contract_cols(query_raw_grad, qup_mat)
    qup_term = contract_rows(query_all, raw_all).astype(BF)
    qdown_grad = rms_query * (
        query_in_grad
        - normed_query * jnp.mean(query_in_grad * normed_query, axis=-1, keepdims=True)
    )
    kv_grad, qup_term = lax.optimization_barrier((kv_grad, qup_term))
    key_raw_grad = rotate_back(kv_grad[:, :HD], cosine, sine)
    qkv_low = jnp.concatenate([qdown_grad, key_raw_grad, kv_grad[:, HD:]], axis=1).astype(BF)
    qkv_parts, out_ends = lax.optimization_barrier(
        (exchange_group(qkv_low, pick_cols), out_ends)
    )
    out_pre = end_reduce_y(*out_ends)
    out_sum = scatter_z(out_pre)
    qkv_all = jnp.concatenate(after(qkv_parts, out_pre), axis=0)
    qkv_term = contract_rows(input_all, qkv_all).astype(BF)
    n_own = query_down.shape[0]
    qkv_near = small_over_y(
        [
            [
                lax.dynamic_slice_in_dim(qkv_term, position_of(dz, dy) * n_own, n_own)
                for dz in range(Z)
            ]
            for dy in range(n_y)
        ]
    )
    first_part = contract_cols(after(qkv_all, qkv_term), qkv_mat)
    first_in_grad = reduce_group(split(first_part))
    qup_ends = begin_reduce_y(after(qup_term, out_ends))
    layer_part = matmul(after(hidden_low, first_part), down_mat)
    down_sum = reduce_own_y(after(down_half, layer_part))
    up_sum = reduce_own_y(after(up_half, down_half))
    qup_ends, first_in_grad, layer_part, up_sum = lax.optimization_barrier(
        (qup_ends, first_in_grad, layer_part, up_sum)
    )
    qup_pre = end_reduce_y(*qup_ends)
    qup_sum = scatter_z(qup_pre)
    layer_sum = reduce_group(split(layer_part))
    up_slots = gather_group(up_sum)
    gate_slots = gather_group(after(gate_sum, up_sum))
    down_slots = gather_group(down_sum)
    qkv_blocks = small_over_z(qkv_near)
    qkv_blocks, up_slots, gate_slots = lax.optimization_barrier(
        (qkv_blocks, up_slots, gate_slots)
    )
    input_rows_grad = middle_grad + rms_first * (
        first_in_grad
        - normed_first * jnp.mean(first_in_grad * normed_first, axis=-1, keepdims=True)
    )
    order = jnp.zeros((n_group,), jnp.int32)
    for k, (dc, dx) in enumerate(offsets()):
        order = order.at[member_of(dc, dx)].set(k)
    gateup_grad, second_gain_grad = interleave(
        order, mlp_gain.astype(F32)[:, None], gate_up, gate_slots, up_slots, n_shard
    )
    qkv_blocks, gateup_grad, layer_sum, down_slots = lax.optimization_barrier(
        (qkv_blocks, gateup_grad, layer_sum, down_slots)
    )
    qkv_sum = added(qkv_blocks).astype(BF)
    layer = (middle + layer_sum) * valid
    out_slots = gather_group(after(out_sum, gate_slots))

    down_grad = place_group(down_slots, 0, F32)
    out_grad = place_group(out_slots, 0, F32)
    qup_raw = place_group(gather_group(after(qup_sum, out_slots)), 1, F32)
    qkv_raw = place_group(gather_group(qkv_sum), 1, F32)

    def gain_grad(weight, grad):
        return jnp.sum(weight.astype(F32) * grad, axis=1)

    qkv_weight_grad = qkv_raw * attn_gain.astype(F32)[:, None]
    return (
        layer.astype(BF)[None],
        input_rows_grad.astype(BF)[None],
        gain_grad(qkv_own, qkv_raw),
        qkv_weight_grad[:, :rank],
        qkv_weight_grad[:, rank:],
        gain_grad(query_up, qup_raw),
        qup_raw * query_gain.astype(F32)[:, None],
        out_grad,
        second_gain_grad[:, 0],
        gateup_grad,
        down_grad,
    )


def solution(mesh):
    n_replica, n_shard = mesh.devices.shape
    devices = mesh.devices.reshape(n_replica // CORES, CORES, Z, n_shard // Z)
    inner = Mesh(devices, ("x", "c", "z", "y"))
    group, shard = ("x", "c"), ("z", "y")
    acts = P(group, shard, None)
    vec = P(shard)
    mat = P(shard, None)
    in_specs = (acts, acts, P(), vec, mat, mat, vec, mat, mat, vec, mat, mat)
    out_specs = (acts, acts, vec, mat, mat, vec, mat, mat, vec, mat, mat)
    return jax.shard_map(
        on_device, mesh=inner, in_specs=in_specs, out_specs=out_specs, check_vma=False
    )
```

```python
import math

import jax
import jax.numpy as jnp
from jax import lax
from jax.experimental import pallas as pl
from jax.experimental.pallas import tpu as pltpu
from jax.sharding import Mesh
from jax.sharding import PartitionSpec as P

HEADS = 16
HD = 256
FF = 5632
Z = 4
CORES = 2


EPSILON = 1e-06
BF = jnp.bfloat16
F32 = jnp.float32


def inv_rms(values):
    return lax.rsqrt(jnp.mean(values * values, axis=-1, keepdims=True) + EPSILON)


def rope_tables(positions, head_dim):
    half_dim = head_dim // 2
    frequency = jnp.exp(-math.log(10000.0) * jnp.arange(half_dim).astype(F32) / half_dim)
    angles = positions.astype(F32)[:, None] * frequency[None, :]
    return (jnp.cos(angles), jnp.sin(angles))


def rotate(values, cosine, sine):
    half_dim = values.shape[-1] // 2
    first_half = values[..., :half_dim]
    second_half = values[..., half_dim:]
    return jnp.concatenate(
        [first_half * cosine - second_half * sine, second_half * cosine + first_half * sine],
        axis=-1,
    )


def rotate_back(grads, cosine, sine):
    half_dim = grads.shape[-1] // 2
    first_half = grads[..., :half_dim]
    second_half = grads[..., half_dim:]
    return jnp.concatenate(
        [first_half * cosine + second_half * sine, second_half * cosine - first_half * sine],
        axis=-1,
    )


def matmul(left, right):
    return jnp.dot(left, right, preferred_element_type=F32)


def contract_rows(left, right):
    return lax.dot_general(left, right, (((0,), (0,)), ((), ())), preferred_element_type=F32)


def contract_cols(left, right):
    return lax.dot_general(left, right, (((1,), (1,)), ((), ())), preferred_element_type=F32)


STEP_HEADS = 4
LIGHT = 1000
NEG = -1e30


def dot_last(left, right):
    return lax.dot_general(left, right, (((1,), (1,)), ((), ())), preferred_element_type=F32)


def seen(shape, rows, y_index):
    n_y = shape[0] // rows
    key = lax.broadcasted_iota(jnp.int32, shape, 0)
    row = lax.broadcasted_iota(jnp.int32, shape, 1)
    ahead = key // rows
    block = lax.rem(y_index + ahead, n_y)
    return (block - y_index) * rows + key - ahead * rows <= row


def attend_kernel(
    place_ref, input_ref, up_ref, cos_ref, sin_ref, kv_ref, q_ref, o_ref, lse_ref,
    vt_ref, m_ref, l_ref, acc_ref,
):
    rows = input_ref.shape[0]
    chunk_rows = kv_ref.shape[0] // Z
    half = HD // 2

    @pl.when(pl.program_id(0) == 0)
    def _():
        for c in range(Z):
            at = slice(c * chunk_rows, (c + 1) * chunk_rows)
            vt_ref[:, at] = kv_ref[at, HD:].T

    cosine, sine = cos_ref[...], sin_ref[...]
    scale = 1.0 / math.sqrt(HD)
    raw = matmul(input_ref[...], up_ref[...])
    for j in range(STEP_HEADS):
        first, second = raw[:, j * HD : j * HD + half], raw[:, j * HD + half : (j + 1) * HD]
        turned = jnp.concatenate(
            [first * cosine - second * sine, second * cosine + first * sine], axis=1
        )
        q_ref[:, j * HD : (j + 1) * HD] = (turned.astype(BF).astype(F32) * scale).astype(BF)
    m_ref[...] = jnp.full_like(m_ref, NEG)
    l_ref[...] = jnp.zeros_like(l_ref)
    acc_ref[...] = jnp.zeros_like(acc_ref)

    def chunk(c, masked):
        at = pl.multiple_of(c * chunk_rows, chunk_rows)
        keys = kv_ref[pl.ds(at, chunk_rows), :HD]
        values = vt_ref[:, pl.ds(at, chunk_rows)]
        for j in range(STEP_HEADS):
            scores = dot_last(keys, q_ref[:, j * HD : (j + 1) * HD])
            if masked:
                scores = jnp.where(seen(scores.shape, rows, place_ref[1]), scores, NEG)
            peak = jnp.maximum(m_ref[j], jnp.max(scores, axis=0, keepdims=True))
            alpha = jnp.exp(m_ref[j] - peak)
            expo = jnp.exp(scores - peak)
            m_ref[j] = peak
            l_ref[j] = l_ref[j] * alpha + jnp.sum(expo, axis=0, keepdims=True)
            acc_ref[j] = acc_ref[j] * alpha + matmul(values, expo.astype(BF))

    @pl.loop(Z - place_ref[0], Z)
    def _(c):
        chunk(c, False)

    chunk(0, True)
    for j in range(STEP_HEADS):
        o_ref[:, j * HD : (j + 1) * HD] = (acc_ref[j] / l_ref[j]).T.astype(BF)
        lse_ref[j] = m_ref[j] + jnp.log(l_ref[j])


def attend(place, query_input, up_mat, cosine, sine, kv_whole):
    rows, rank = query_input.shape
    slot_len = kv_whole.shape[0]
    wide = STEP_HEADS * HD
    whole = lambda h, *_: (0, 0)
    by_head = lambda h, *_: (0, h)
    return pl.pallas_call(
        attend_kernel,
        out_shape=(
            jax.ShapeDtypeStruct((rows, HEADS * HD), BF),
            jax.ShapeDtypeStruct((rows, HEADS * HD), BF),
            jax.ShapeDtypeStruct((HEADS, 1, rows), F32),
        ),
        grid_spec=pltpu.PrefetchScalarGridSpec(
            num_scalar_prefetch=1,
            grid=(HEADS // STEP_HEADS,),
            in_specs=[
                pl.BlockSpec((rows, rank), whole),
                pl.BlockSpec((rank, wide), by_head),
                pl.BlockSpec((rows, HD // 2), whole),
                pl.BlockSpec((rows, HD // 2), whole),
                pl.BlockSpec((slot_len, 2 * HD), whole),
            ],
            out_specs=[
                pl.BlockSpec((rows, wide), by_head),
                pl.BlockSpec((rows, wide), by_head),
                pl.BlockSpec((STEP_HEADS, 1, rows), lambda h, *_: (h, 0, 0)),
            ],
            scratch_shapes=[
                pltpu.VMEM((HD, slot_len), BF),
                pltpu.VMEM((STEP_HEADS, 1, rows), F32),
                pltpu.VMEM((STEP_HEADS, 1, rows), F32),
                pltpu.VMEM((STEP_HEADS, HD, rows), F32),
            ],
        ),
        compiler_params=pltpu.CompilerParams(
            dimension_semantics=("arbitrary",), vmem_limit_bytes=40 * 1024 * 1024
        ),
        cost_estimate=pl.CostEstimate(
            flops=LIGHT, bytes_accessed=LIGHT, transcendentals=0
        ),
    )(place, query_input, up_mat, cosine, sine, kv_whole)


def attend_back_kernel(
    place_ref, q_ref, do_ref, o_ref, lse_ref, cos_ref, sin_ref, kv_ref, dq_ref, dkv_ref,
    acc_ref, dqs_ref,
):
    rows = q_ref.shape[0]
    chunk_rows = kv_ref.shape[0] // Z
    half = HD // 2
    step = pl.program_id(0)

    @pl.when(step == 0)
    def _():
        acc_ref[...] = jnp.zeros_like(acc_ref)

    dqs_ref[...] = jnp.zeros_like(dqs_ref)
    deltas = []
    for j in range(STEP_HEADS):
        at = slice(j * HD, (j + 1) * HD)
        prod = do_ref[:, at].astype(F32) * o_ref[:, at].astype(F32)
        deltas.append(jnp.sum(prod.T, axis=0, keepdims=True))

    def chunk(c, masked):
        at = pl.ds(pl.multiple_of(c * chunk_rows, chunk_rows), chunk_rows)
        keys = kv_ref[at, :HD]
        values = kv_ref[at, HD:]
        weights = []
        for j in range(STEP_HEADS):
            query = q_ref[:, j * HD : (j + 1) * HD]
            out_grad = do_ref[:, j * HD : (j + 1) * HD]
            probs = jnp.exp(dot_last(keys, query) - lse_ref[j])
            if masked:
                probs = jnp.where(seen(probs.shape, rows, place_ref[1]), probs, 0.0)
            score_grad = (probs * (dot_last(values, out_grad) - deltas[j])).astype(BF)
            dqs_ref[j] += contract_rows(score_grad, keys)
            weights.append((probs.astype(BF), score_grad, out_grad, query))
        prob_rows, grad_rows, out_grads, queries = zip(*weights)
        acc_ref[at, HD:] += matmul(
            jnp.concatenate(prob_rows, axis=1), jnp.concatenate(out_grads, axis=0)
        )
        acc_ref[at, :HD] += matmul(
            jnp.concatenate(grad_rows, axis=1), jnp.concatenate(queries, axis=0)
        )

    @pl.loop(Z - place_ref[0], Z)
    def _(c):
        chunk(c, False)

    chunk(0, True)
    cosine, sine = cos_ref[...], sin_ref[...]
    scale = 1.0 / math.sqrt(HD)
    for j in range(STEP_HEADS):
        first, second = dqs_ref[j, :, :half] * scale, dqs_ref[j, :, half:] * scale
        dq_ref[:, j * HD : (j + 1) * HD] = jnp.concatenate(
            [first * cosine + second * sine, second * cosine - first * sine], axis=1
        ).astype(BF)

    @pl.when(step == pl.num_programs(0) - 1)
    def _():
        dkv_ref[...] = acc_ref[...].astype(BF)


def attend_back(place, query, out_grad, attn_low, logsum, cosine, sine, kv_whole):
    rows = query.shape[0]
    slot_len = kv_whole.shape[0]
    wide = STEP_HEADS * HD
    whole = lambda h, *_: (0, 0)
    by_head = lambda h, *_: (0, h)
    return pl.pallas_call(
        attend_back_kernel,
        out_shape=(
            jax.ShapeDtypeStruct((rows, HEADS * HD), BF),
            jax.ShapeDtypeStruct((slot_len, 2 * HD), BF),
        ),
        grid_spec=pltpu.PrefetchScalarGridSpec(
            num_scalar_prefetch=1,
            grid=(HEADS // STEP_HEADS,),
            in_specs=[
                pl.BlockSpec((rows, wide), by_head),
                pl.BlockSpec((rows, wide), by_head),
                pl.BlockSpec((rows, wide), by_head),
                pl.BlockSpec((STEP_HEADS, 1, rows), lambda h, *_: (h, 0, 0)),
                pl.BlockSpec((rows, HD // 2), whole),
                pl.BlockSpec((rows, HD // 2), whole),
                pl.BlockSpec((slot_len, 2 * HD), whole),
            ],
            out_specs=[
                pl.BlockSpec((rows, wide), by_head),
                pl.BlockSpec((slot_len, 2 * HD), whole),
            ],
            scratch_shapes=[
                pltpu.VMEM((slot_len, 2 * HD), F32),
                pltpu.VMEM((STEP_HEADS, rows, HD), F32),
            ],
        ),
        compiler_params=pltpu.CompilerParams(
            dimension_semantics=("arbitrary",), vmem_limit_bytes=40 * 1024 * 1024
        ),
        cost_estimate=pl.CostEstimate(
            flops=LIGHT, bytes_accessed=LIGHT, transcendentals=0
        ),
    )(place, query, out_grad, attn_low, logsum, cosine, sine, kv_whole)


def interleave_kernel(n_shard, order_ref, gain_ref, weight_ref, *refs):
    *slot_refs, out_ref, sum_ref = refs
    n_group = len(slot_refs) // 2
    part = slot_refs[0].shape[1]
    unit = part // n_shard
    width = part * n_group
    total = 0.0
    gain = gain_ref[...]
    for half in range(2):
        slots = [ref[...].astype(F32) for ref in slot_refs[half * n_group : (half + 1) * n_group]]
        blocks = []
        for member in range(n_group):
            block = slots[0]
            for k in range(1, n_group):
                block = jnp.where(order_ref[member] == k, slots[k], block)
            blocks.append(block)
        row = jnp.concatenate(
            [
                blocks[member][:, s * unit : (s + 1) * unit]
                for s in range(n_shard)
                for member in range(n_group)
            ],
            axis=1,
        )
        at = slice(half * width, (half + 1) * width)
        total = total + jnp.sum(row * weight_ref[:, at].astype(F32), axis=1, keepdims=True)
        out_ref[:, at] = row * gain
    sum_ref[...] = total


def interleave(order, gain, weight, gate_slots, up_slots, n_shard):
    rows, width = weight.shape
    block = 32
    slots = [*gate_slots, *up_slots]
    by_row = lambda i, *_: (i, 0)
    return pl.pallas_call(
        lambda *refs: interleave_kernel(n_shard, *refs),
        out_shape=(
            jax.ShapeDtypeStruct((rows, width), F32),
            jax.ShapeDtypeStruct((rows, 1), F32),
        ),
        grid_spec=pltpu.PrefetchScalarGridSpec(
            num_scalar_prefetch=1,
            grid=(rows // block,),
            in_specs=[
                pl.BlockSpec((block, 1), by_row),
                pl.BlockSpec((block, width), by_row),
                *[pl.BlockSpec((block, slots[0].shape[1]), by_row) for _ in slots],
            ],
            out_specs=[
                pl.BlockSpec((block, width), by_row),
                pl.BlockSpec((block, 1), by_row),
            ],
        ),
        compiler_params=pltpu.CompilerParams(dimension_semantics=("arbitrary",)),
        cost_estimate=pl.CostEstimate(flops=LIGHT, bytes_accessed=LIGHT, transcendentals=0),
    )(order, gain, weight, *slots)


def select_kernel(n_shard, n_group, member_ref, gain_ref, weight_ref, gate_ref, up_ref):
    width = weight_ref.shape[1] // 2
    unit = width // n_shard // n_group
    gain = gain_ref[...]
    for half, out_ref in enumerate((gate_ref, up_ref)):
        pieces = []
        for s in range(n_shard):
            at = half * width + s * n_group * unit
            piece = weight_ref[:, at : at + unit].astype(F32)
            for k in range(1, n_group):
                other = weight_ref[:, at + k * unit : at + (k + 1) * unit].astype(F32)
                piece = jnp.where(member_ref[0] == k, other, piece)
            pieces.append(piece)
        out_ref[...] = (jnp.concatenate(pieces, axis=1) * gain).astype(BF)


def select_units(member, gain, weight, n_shard, n_group):
    rows, width = weight.shape
    block = 32
    part = width // 2 // n_group
    by_row = lambda i, *_: (i, 0)
    return pl.pallas_call(
        lambda *refs: select_kernel(n_shard, n_group, *refs),
        out_shape=(jax.ShapeDtypeStruct((rows, part), BF),) * 2,
        grid_spec=pltpu.PrefetchScalarGridSpec(
            num_scalar_prefetch=1,
            grid=(rows // block,),
            in_specs=[
                pl.BlockSpec((block, 1), by_row),
                pl.BlockSpec((block, width), by_row),
            ],
            out_specs=[pl.BlockSpec((block, part), by_row)] * 2,
        ),
        compiler_params=pltpu.CompilerParams(dimension_semantics=("arbitrary",)),
        cost_estimate=pl.CostEstimate(flops=LIGHT, bytes_accessed=LIGHT, transcendentals=0),
    )(member, gain, weight)


def from_ahead(value, axis, step):
    n = lax.axis_size(axis)
    return lax.ppermute(value, axis, [((j + step) % n, j) for j in range(n)])


def to_ahead(value, axis, step):
    n = lax.axis_size(axis)
    return lax.ppermute(value, axis, [(j, (j + step) % n) for j in range(n)])


def gather_group(value):
    n_x = lax.axis_size("x")
    mine = [value] + [from_ahead(value, "x", k) for k in range(1, n_x)]
    return mine + [from_ahead(v, "c", 1) for v in mine]


def reduce_group(parts):
    n_x = lax.axis_size("x")
    near, far = parts[:n_x], parts[n_x:]
    sums = [a + to_ahead(b.astype(BF), "c", 1).astype(F32) for a, b in zip(near, far)]
    total = sums[0]
    for k in range(1, n_x):
        total = total + to_ahead(sums[k].astype(BF), "x", k).astype(F32)
    return total


def exchange_group(value, pick):
    n_x = lax.axis_size("x")
    x_id, c_id = lax.axis_index("x"), lax.axis_index("c")
    out = []
    for dc in range(CORES):
        for dx in range(n_x):
            member = lax.rem(x_id + n_x - dx, n_x) * CORES + lax.rem(c_id + dc, CORES)
            block = pick(value, member)
            if dx or dc:
                perm = []
                for j in range(n_x):
                    for c in range(CORES):
                        source = ((j + dx) % n_x) * CORES + (c + dc) % CORES
                        perm.append((source, j * CORES + c))
                block = lax.ppermute(block, ("x", "c"), perm)
            out.append(block)
    return out


def shard_offsets():
    return [(dz, dy) for dz in range(Z) for dy in range(lax.axis_size("y"))]


def shard_permute(value, dz, dy, ahead):
    n_y = lax.axis_size("y")
    perm = []
    for z in range(Z):
        for y in range(n_y):
            far, near = ((z + dz) % Z) * n_y + (y + dy) % n_y, z * n_y + y
            perm.append((near, far) if ahead else (far, near))
    return lax.ppermute(value, ("z", "y"), perm)


def position_of(dz, dy):
    n_y = lax.axis_size("y")
    return lax.rem(lax.axis_index("z") + dz, Z) * n_y + lax.rem(lax.axis_index("y") + dy, n_y)


def ring_z(value):
    return [from_ahead(value, "z", k) if k else value for k in range(Z)]


def small_over_y(blocks):
    total = jnp.stack(blocks[0]).astype(F32)
    for k, group in enumerate(blocks[1:]):
        total = total + to_ahead(jnp.stack(group).astype(BF), "y", k + 1).astype(F32)
    return total


def small_over_z(total):
    low = total.astype(BF)
    return [total[0]] + [to_ahead(low[k], "z", k) for k in range(1, Z)]


def added(blocks):
    total = blocks[0]
    for block in blocks[1:]:
        total = total + block.astype(F32)
    return total


def after(values, done):
    return lax.optimization_barrier((values, done))[0]


def gather_z(value):
    return lax.all_gather(value, "z", axis=0, tiled=True)


def gather_shard(value):
    return lax.all_gather(value, ("z", "y"), axis=0, tiled=True)


def scatter_z(value):
    return lax.psum_scatter(value, "z", scatter_dimension=0, tiled=True)


def begin_reduce_y(value):
    n_y = lax.axis_size("y")
    index = lax.axis_index("y")
    blocks = value.astype(BF).reshape(Z, n_y, -1, value.shape[1])
    own = lax.dynamic_index_in_dim(blocks, index, axis=1, keepdims=False)
    others = []
    for k in range(1, n_y):
        block = lax.dynamic_index_in_dim(blocks, lax.rem(index + k, n_y), axis=1, keepdims=False)
        others.append(to_ahead(block, "y", k))
    return own, others


def end_reduce_y(own, others):
    total = own.astype(F32)
    for block in others:
        total = total + block.astype(F32)
    return total.astype(BF).reshape(-1, own.shape[-1])


def swap_y(wide):
    n_y = lax.axis_size("y")
    return [wide] + [from_ahead(wide, "y", k) for k in range(1, n_y)]


def merge_y(blocks, n):
    n_y = lax.axis_size("y")
    m = blocks[0].shape[1]
    blocks = [block.reshape(Z, 1, n, m) for block in blocks]
    if n_y == 2:
        first, second = blocks
        return jnp.where(
            lax.axis_index("y") == 0,
            jnp.concatenate([first, second], axis=1),
            jnp.concatenate([second, first], axis=1),
        ).reshape(-1, m)
    at = lax.rem(n_y - lax.axis_index("y"), n_y)
    stacked = jnp.concatenate(blocks + blocks[:-1], axis=1)
    return lax.dynamic_slice_in_dim(stacked, at, n_y, axis=1).reshape(-1, m)


def merge_own_y(blocks):
    n_y = lax.axis_size("y")
    if n_y == 2:
        first, second = blocks
        return jnp.where(
            lax.axis_index("y") == 0,
            jnp.concatenate([first, second]),
            jnp.concatenate([second, first]),
        )
    n = blocks[0].shape[0]
    at = lax.rem(n_y - lax.axis_index("y"), n_y) * n
    return lax.dynamic_slice_in_dim(jnp.concatenate(blocks + blocks[:-1]), at, n_y * n)


def reduce_own_y(value):
    n_y = lax.axis_size("y")
    index = lax.axis_index("y")
    blocks = value.reshape(n_y, -1, value.shape[1])
    total = lax.dynamic_index_in_dim(blocks, index, keepdims=False).astype(F32)
    for k in range(1, n_y):
        other = lax.dynamic_index_in_dim(blocks, lax.rem(index + k, n_y), keepdims=False)
        total = total + to_ahead(other, "y", k).astype(F32)
    return total.astype(BF)


def member_of(dc, dx):
    n_x = lax.axis_size("x")
    x_id = lax.rem(lax.axis_index("x") + dx, n_x)
    return x_id * CORES + lax.rem(lax.axis_index("c") + dc, CORES)


def offsets():
    return [(dc, dx) for dc in range(CORES) for dx in range(lax.axis_size("x"))]


def place_group(slots, axis, dtype):
    n = slots[0].shape[axis]
    shape = list(slots[0].shape)
    shape[axis] = n * len(slots)
    out = jnp.zeros(shape, dtype)
    for (dc, dx), slot in zip(offsets(), slots):
        start = [0] * len(shape)
        start[axis] = member_of(dc, dx) * n
        out = lax.dynamic_update_slice(out, slot.astype(dtype), start)
    return out


def spread_begin(wide):
    n_y, n_x = lax.axis_size("y"), lax.axis_size("x")
    over_y = [wide] + [from_ahead(wide, "y", k) for k in range(1, n_y)]
    over_x = [from_ahead(wide, "x", k) for k in range(1, n_x)]
    return over_y, over_x


def spread_next(over_y, over_x):
    n_x = lax.axis_size("x")
    return [[over_y[0]] + over_x] + [
        [block] + [from_ahead(block, "x", k) for k in range(1, n_x)] for block in over_y[1:]
    ]


def spread_end(grid):
    return [group + [from_ahead(block, "c", 1) for block in group] for group in grid]


def place_every(slots, n):
    n_y, n_x = lax.axis_size("y"), lax.axis_size("x")
    m = slots[0][0].shape[1]
    out = jnp.zeros((Z, n_y, n_x * CORES, n, m), BF)
    for ky, group in enumerate(slots):
        at_y = lax.rem(lax.axis_index("y") + ky, n_y)
        for (dc, dx), slot in zip(offsets(), group):
            out = lax.dynamic_update_slice(
                out, slot.reshape(Z, 1, 1, n, m), (0, at_y, member_of(dc, dx), 0, 0)
            )
    return out.reshape(-1, m)


def on_device(
    tokens,
    cotangent,
    lengths,
    attn_gain,
    query_down,
    key_value,
    query_gain,
    query_up,
    out_proj,
    mlp_gain,
    gate_up,
    down_proj,
):
    n_x = lax.axis_size("x")
    n_group = n_x * CORES
    n_y = lax.axis_size("y")
    n_shard = Z * n_y
    _, rows, width = tokens.shape
    rank = query_down.shape[1]
    group_id = lax.axis_index("x") * CORES + lax.axis_index("c")
    shard_id = lax.axis_index("z") * n_y + lax.axis_index("y")

    def quarter_rows(value):
        n = value.shape[0] // n_group
        return lax.dynamic_slice_in_dim(value, group_id * n, n, axis=0)

    def pick_cols(value, member):
        n = value.shape[1] // n_group
        return lax.dynamic_slice_in_dim(value, member * n, n, axis=1)

    def scaled(weight, gain):
        return (weight.astype(F32) * gain.astype(F32)[:, None]).astype(BF)

    def split(value):
        return [value[k * rows : (k + 1) * rows] for k in range(n_group)]

    qkv_own = jnp.concatenate([query_down, key_value], axis=1)
    qkv_ring = ring_z(scaled(pick_cols(qkv_own, group_id), attn_gain))
    qup_own = quarter_rows(scaled(query_up, query_gain))
    qup_mat = lax.all_gather(qup_own, ("z", "y", "x", "c"), axis=0, tiled=True)
    out_wide = gather_z(quarter_rows(out_proj))

    my_length = lax.dynamic_index_in_dim(lengths, group_id, keepdims=False)
    positions = shard_id * rows + jnp.arange(rows, dtype=jnp.int32)
    place = jnp.stack([lax.axis_index("z"), lax.axis_index("y")]).astype(jnp.int32)
    valid = (positions < my_length).astype(F32)[:, None]
    cosine, sine = rope_tables(positions, HD)

    x_rows = tokens[0].astype(F32)
    rms_first = inv_rms(x_rows)
    normed_first = x_rows * rms_first
    attn_input = normed_first.astype(BF)
    input_all = jnp.concatenate(gather_group(attn_input), axis=0)

    qkv_stack = jnp.stack(qkv_ring)
    qkv_grid = [qkv_stack] + [from_ahead(qkv_stack, "y", k) for k in range(1, n_y)]

    gate_up_late = after(gate_up, qkv_ring[1])
    gate_own, up_own = select_units(
        group_id.astype(jnp.int32).reshape(1),
        mlp_gain.astype(F32)[:, None],
        gate_up_late,
        n_shard,
        n_group,
    )
    gate_wide = gather_z(gate_own)

    qkv_mat = jnp.zeros((width, qkv_stack.shape[2]), BF)
    for dy, stack in enumerate(qkv_grid):
        for dz in range(Z):
            at = position_of(dz, dy) * stack.shape[1]
            qkv_mat = lax.dynamic_update_slice(qkv_mat, stack[dz], (at, 0))
    qkv_flat = matmul(input_all, qkv_mat)
    up_wide = gather_z(up_own)
    blocks = []
    for (dc, dx), block in zip(offsets(), split(qkv_flat)):
        if dc or dx:
            perm = []
            for j in range(n_x):
                for c in range(CORES):
                    target = ((j + dx) % n_x) * CORES + (c + dc) % CORES
                    perm.append((j * CORES + c, target))
            block = lax.ppermute(block, ("x", "c"), perm)
        blocks.append(block)
    qkv_out = jnp.zeros((rows, qkv_own.shape[1]), F32)
    n_cols = qkv_own.shape[1] // n_group
    for (dc, dx), block in zip(offsets(), blocks):
        member = lax.rem(lax.axis_index("x") + n_x - dx, n_x) * CORES
        member = member + lax.rem(lax.axis_index("c") + dc, CORES)
        qkv_out = lax.dynamic_update_slice(qkv_out, block, (0, member * n_cols))
    qdown_out, kv_out = qkv_out[:, :rank], qkv_out[:, rank:]

    key_rot = rotate(kv_out[:, :HD], cosine, sine).astype(BF)
    kv_local = jnp.concatenate([key_rot, kv_out[:, HD:].astype(BF)], axis=1)
    out_first = spread_begin(out_wide)
    kv_local = after(kv_local, out_wide)
    kv_ring = ring_z(kv_local)
    down_both = [quarter_rows(down_proj)]
    down_both += [from_ahead(after(down_both[0], qkv_flat), "y", k) for k in range(1, n_y)]
    down_mat = gather_z(merge_own_y(down_both))
    rms_query = inv_rms(qdown_out)
    normed_query = qdown_out * rms_query
    query_input = normed_query.astype(BF)
    kv_stack = jnp.stack(kv_ring)
    kv_grid = [kv_stack] + [from_ahead(kv_stack, "y", k) for k in range(1, n_y)]
    kv_grid = after(kv_grid, out_first)
    kv_whole = jnp.concatenate([stack[dz] for dz in range(Z) for stack in kv_grid])
    out_grid = spread_next(*out_first)
    query_rot, attn_low, logsum = attend(place, query_input, qup_mat, cosine, sine, kv_whole)
    gate_blocks = swap_y(gate_wide)
    out_slots = spread_end(after(out_grid, attn_low))
    out_mat = place_every(out_slots, out_proj.shape[0] // n_group)
    middle = x_rows + matmul(attn_low, out_mat)
    rms_second = inv_rms(middle)
    normed_second = middle * rms_second
    mlp_input = normed_second.astype(BF)

    mlp_all = jnp.concatenate(gather_group(mlp_input), axis=0)
    up_blocks = swap_y(up_wide)
    cot_rows = cotangent[0].astype(F32) * valid
    cot_late = after(cot_rows.astype(BF), mlp_input)
    cot_all = jnp.concatenate(gather_group(cot_late), axis=0)
    gate_mat = merge_y(after(gate_blocks, mlp_all), mlp_gain.shape[0])
    gate_part = matmul(mlp_all, gate_mat)
    up_mat = merge_y(after(up_blocks, (gate_part, down_mat)), mlp_gain.shape[0])
    def pick_out(value, member):
        parts = value.reshape(rows, n_shard, n_group, -1)
        return lax.dynamic_index_in_dim(parts, member, axis=2, keepdims=False).reshape(rows, -1)

    attn_late, query_late = after((attn_low, query_input), mlp_all)
    attn_all = jnp.concatenate(exchange_group(attn_late, pick_out), axis=0)
    query_all = jnp.concatenate(gather_group(query_late), axis=0)

    up_mat, attn_all, query_all = lax.optimization_barrier((up_mat, attn_all, query_all))
    up_part = matmul(mlp_all, up_mat)
    sigmoid_gate = jax.nn.sigmoid(gate_part)
    activated = gate_part * sigmoid_gate
    hidden_low = (activated * up_part).astype(BF)

    down_term = contract_rows(hidden_low, cot_all).astype(BF)
    down_half = scatter_z(down_term)
    down_mat = after(down_mat, down_term)
    hidden_grad = contract_cols(cot_all, down_mat)
    gate_grad = hidden_grad * up_part * (sigmoid_gate * (1.0 + gate_part * (1.0 - sigmoid_gate)))
    gate_low = gate_grad.astype(BF)
    up_low = (hidden_grad * activated).astype(BF)
    partial_in = contract_cols(gate_low, gate_mat) + contract_cols(up_low, up_mat)
    gate_low, up_low = after((gate_low, up_low), partial_in)
    gate_term = contract_rows(mlp_all, gate_low).astype(BF)
    gate_ends = begin_reduce_y(gate_term)
    up_term = contract_rows(mlp_all, after(up_low, gate_term)).astype(BF)
    up_half = scatter_z(up_term)
    mlp_in_grad = after(reduce_group(split(partial_in)), up_term)

    middle_grad = cot_rows + rms_second * (
        mlp_in_grad
        - normed_second * jnp.mean(mlp_in_grad * normed_second, axis=-1, keepdims=True)
    )
    middle_low = middle_grad.astype(BF)
    middle_all = jnp.concatenate(gather_group(middle_low), axis=0)
    attn_val_grad = contract_cols(middle_low, out_mat).astype(BF)
    query_raw_grad, kv_term = attend_back(
        place, query_rot, attn_val_grad, attn_low, logsum, cosine, sine, kv_whole
    )
    kv_slots = [kv_term[k * rows : (k + 1) * rows] for k in range(Z * n_y)]
    kv_near = small_over_y([kv_slots[k::n_y] for k in range(n_y)])
    kv_blocks = small_over_z(kv_near)
    gate_pre = end_reduce_y(gate_ends[0], after(gate_ends[1], kv_term))
    gate_sum = scatter_z(gate_pre)
    out_term = contract_rows(attn_all, after(middle_all, gate_pre)).astype(BF)
    out_ends = begin_reduce_y(out_term)
    kv_blocks, out_term = lax.optimization_barrier((kv_blocks, out_term))
    kv_grad = added(kv_blocks)
    raw_all = jnp.concatenate(exchange_group(query_raw_grad, pick_cols), axis=0)
    query_in_grad = contract_cols(query_raw_grad, qup_mat)
    qup_term = contract_rows(query_all, raw_all).astype(BF)
    qdown_grad = rms_query * (
        query_in_grad
        - normed_query * jnp.mean(query_in_grad * normed_query, axis=-1, keepdims=True)
    )
    kv_grad, qup_term = lax.optimization_barrier((kv_grad, qup_term))
    key_raw_grad = rotate_back(kv_grad[:, :HD], cosine, sine)
    qkv_low = jnp.concatenate([qdown_grad, key_raw_grad, kv_grad[:, HD:]], axis=1).astype(BF)
    qkv_parts, out_ends = lax.optimization_barrier(
        (exchange_group(qkv_low, pick_cols), out_ends)
    )
    out_pre = end_reduce_y(*out_ends)
    out_sum = scatter_z(out_pre)
    qkv_all = jnp.concatenate(after(qkv_parts, out_pre), axis=0)
    qkv_term = contract_rows(input_all, qkv_all).astype(BF)
    n_own = query_down.shape[0]
    qkv_near = small_over_y(
        [
            [
                lax.dynamic_slice_in_dim(qkv_term, position_of(dz, dy) * n_own, n_own)
                for dz in range(Z)
            ]
            for dy in range(n_y)
        ]
    )
    first_part = contract_cols(after(qkv_all, qkv_term), qkv_mat)
    first_in_grad = reduce_group(split(first_part))
    qup_ends = begin_reduce_y(after(qup_term, out_ends))
    layer_part = matmul(after(hidden_low, first_part), down_mat)
    down_sum = reduce_own_y(after(down_half, layer_part))
    up_sum = reduce_own_y(after(up_half, down_half))
    qup_ends, first_in_grad, layer_part, up_sum = lax.optimization_barrier(
        (qup_ends, first_in_grad, layer_part, up_sum)
    )
    qup_pre = end_reduce_y(*qup_ends)
    qup_sum = scatter_z(qup_pre)
    layer_sum = reduce_group(split(layer_part))
    up_slots = gather_group(up_sum)
    gate_slots = gather_group(after(gate_sum, up_sum))
    down_slots = gather_group(down_sum)
    qkv_blocks = small_over_z(qkv_near)
    qkv_blocks, up_slots, gate_slots = lax.optimization_barrier(
        (qkv_blocks, up_slots, gate_slots)
    )
    input_rows_grad = middle_grad + rms_first * (
        first_in_grad
        - normed_first * jnp.mean(first_in_grad * normed_first, axis=-1, keepdims=True)
    )
    order = jnp.zeros((n_group,), jnp.int32)
    for k, (dc, dx) in enumerate(offsets()):
        order = order.at[member_of(dc, dx)].set(k)
    gateup_grad, second_gain_grad = interleave(
        order, mlp_gain.astype(F32)[:, None], gate_up, gate_slots, up_slots, n_shard
    )
    qkv_blocks, gateup_grad, layer_sum, down_slots = lax.optimization_barrier(
        (qkv_blocks, gateup_grad, layer_sum, down_slots)
    )
    qkv_sum = added(qkv_blocks).astype(BF)
    layer = (middle + layer_sum) * valid
    out_slots = gather_group(after(out_sum, gate_slots))

    down_grad = place_group(down_slots, 0, F32)
    out_grad = place_group(out_slots, 0, F32)
    qup_raw = place_group(gather_group(after(qup_sum, out_slots)), 1, F32)
    qkv_raw = place_group(gather_group(qkv_sum), 1, F32)

    def gain_grad(weight, grad):
        return jnp.sum(weight.astype(F32) * grad, axis=1)

    qkv_weight_grad = qkv_raw * attn_gain.astype(F32)[:, None]
    return (
        layer.astype(BF)[None],
        input_rows_grad.astype(BF)[None],
        gain_grad(qkv_own, qkv_raw),
        qkv_weight_grad[:, :rank],
        qkv_weight_grad[:, rank:],
        gain_grad(query_up, qup_raw),
        qup_raw * query_gain.astype(F32)[:, None],
        out_grad,
        second_gain_grad[:, 0],
        gateup_grad,
        down_grad,
    )


def solution(mesh):
    n_replica, n_shard = mesh.devices.shape
    devices = mesh.devices.reshape(n_replica // CORES, CORES, Z, n_shard // Z)
    inner = Mesh(devices, ("x", "c", "z", "y"))
    group, shard = ("x", "c"), ("z", "y")
    acts = P(group, shard, None)
    vec = P(shard)
    mat = P(shard, None)
    in_specs = (acts, acts, P(), vec, mat, mat, vec, mat, mat, vec, mat, mat)
    out_specs = (acts, acts, vec, mat, mat, vec, mat, mat, vec, mat, mat)
    return jax.shard_map(
        on_device, mesh=inner, in_specs=in_specs, out_specs=out_specs, check_vma=False
    )
```
